32 devices in a mesh: seq: 8 (over y, x, core), tp: 4 (over z).
Axes of the slice: x: 2, y: 2, z: 4, core: 2. Of those that a mesh axis runs over, the one named last changes fastest.
Arguments:
- grad_out: bfloat16 [1024, 8192], P('seq', 'tp'), may hold values from -6 to 6
- resid_in: bfloat16 [1024, 8192], P('seq', 'tp'), may hold values from -6 to 6
- down_weight: bfloat16 [28672, 8192], P('seq', 'tp'), may hold values from -0.03125 to 0.03125
- hidden_clean: bfloat16 [28672, 512], P('seq', 'tp'), may hold values from -6 to 6
- hidden_corrupt: bfloat16 [28672, 512], P('seq', 'tp'), may hold values from -6 to 6
- patched: int32 [14336], replicated, may hold values from 0 to 28671, as said below
Outputs:
- resid_scores: float32 [1024], P('seq')
- token_scores: float32 [512], P('tp')
- neuron_scores: float32 [28672], P('seq')
The draws below stay inside these ranges and needn't reach their ends.
Inputs may be any that keep to these rules, and one draw needn't show every extreme that they name: `patched`: 14336 distinct hidden-unit indices.
All inputs are finite; a program needn't handle non-finite values.
Results may differ from the reference program's by a relative error of at most 0.0046.
Values may be sent and summed in bfloat16 or wider, within the bound.
A program may use at most 128 MiB of HBM per device.

```python
import math
import jax
import jax.numpy as jnp
from jax import lax

D = 8192
FF = 28672
LEN = 512
NPATCH = 14336


def draw_patched(key, part):
    order = jax.random.permutation(key, FF)
    return order[:NPATCH].astype(jnp.int32)


def levels(key, extent, shards, least, high):
    loudness = 1.0
    for position, shards_of in shards:
        steps = jax.random.uniform(jax.random.fold_in(jax.random.fold_in(key, 6), position), (shards_of,), jnp.float32, least / len(shards), high / len(shards))
        loudness = loudness * jnp.repeat(jnp.exp(steps), extent[position] // shards_of).reshape((-1,) + (1,) * (len(extent) - 1 - position))
    return loudness


def noise(stream_key, extent, scale, bound, pieces=(), held_as=jnp.bfloat16):
    entries = jax.random.normal(stream_key, extent, jnp.float32) * scale
    if len(pieces) > 0:
        entries = levels(stream_key, extent, pieces, -0.22, 0.18) * entries
    return jnp.clip(entries, min=-bound, max=bound).astype(held_as)


def setup_inputs(seed: int = 0) -> dict:
    arg_keys = jax.random.split(jax.random.key(seed), 7)
    return {
        "grad_out": noise(arg_keys[0], (2 * LEN, D), 1.0, 6.0, ((0, 8), (1, 4))),
        "resid_in": noise(arg_keys[1], (2 * LEN, D), 1.0, 6.0, ((0, 8), (1, 4))),
        "down_weight": noise(arg_keys[2], (FF, D), FF ** -0.5, 0.03125, ((0, 8), (1, 4))),
        "hidden_clean": noise(arg_keys[3], (FF, LEN), 1.0, 6.0, ((0, 8), (1, 4))),
        "hidden_corrupt": noise(arg_keys[4], (FF, LEN), 1.0, 6.0, ((0, 8), (1, 4))),
        "patched": draw_patched(jax.random.fold_in(arg_keys[6], 71), 0),
    }


def reference(grad_out, resid_in, down_weight, hidden_clean, hidden_corrupt, patched):
    seq_len = resid_in.shape[0] // 2
    resid_full = resid_in.astype(jnp.float32)
    grad_full = grad_out.astype(jnp.float32)
    resid_diff = resid_full[:seq_len] - resid_full[seq_len:]
    clean_part = lax.optimization_barrier(jnp.sum(resid_diff * grad_full[:seq_len], axis=1))
    corrupt_part = lax.optimization_barrier(jnp.sum(resid_diff * grad_full[seq_len:], axis=1))
    resid_scores = jnp.concatenate([clean_part, corrupt_part]) / math.sqrt(D)
    grad_mean = ((grad_full[:seq_len] + grad_full[seq_len:]) * 0.5).astype(jnp.bfloat16)
    unit_grad = lax.dot_general(down_weight, grad_mean, (((1,), (1,)), ((), ())), preferred_element_type=jnp.float32)
    hidden_diff = (hidden_clean.astype(jnp.float32) - hidden_corrupt.astype(jnp.float32)).astype(jnp.bfloat16)
    product = hidden_diff.astype(jnp.float32) * unit_grad
    in_patch = jnp.zeros((FF,), jnp.float32).at[patched].set(1.0)
    token_scores = lax.optimization_barrier(jnp.sum(product * in_patch[:, None], axis=0)) / math.sqrt(NPATCH)
    neuron_scores = lax.optimization_barrier(jnp.sum(product, axis=1)) / math.sqrt(seq_len)
    return (resid_scores, token_scores, neuron_scores)
```

```python
import functools
import math

import jax
import jax.numpy as jnp
from jax import lax
from jax.experimental import pallas as pl
from jax.experimental.pallas import tpu as pltpu
from jax.sharding import PartitionSpec as P

F32 = jnp.float32
BF16 = jnp.bfloat16
NT = (((1,), (1,)), ((), ()))


def each(count, body):
    def step(index, carry):
        body(index)
        return carry

    lax.fori_loop(0, count, step, 0)


def kernel(
    S, T, C, G, L, K, scales,
    grad_hbm, resid_hbm, weight_hbm, clean_hbm, corrupt_hbm, patched_hbm,
    scores,
    grad, resid, weight, clean, corrupt, patched,
    partner_grad, partner_resid, means, diff, unit, partial, partial_in, mask, acc, token, token_in,
    message, message_in, ending, ending_in, counts, scored, score_out,
    load_sem, piece_sem, weight_sem, pair_send, pair_recv, outer_send, inner_send, mean_recv, diff_send, diff_recv,
    part_send, part_recv, msg_send, msg_recv, end_send, end_recv, tok_send, tok_recv,
):
    seq = lax.axis_index("seq")
    tp = lax.axis_index("tp")
    pairs = S // 2
    partner = lax.rem(seq + pairs, S)
    upper = seq // pairs
    rows = grad.shape[0]
    half = rows // 2
    units = weight.shape[0]
    piece = units // C
    local_len = diff.shape[2]

    lanes = patched.shape[2]
    chunk = rows // K
    barrier = pltpu.get_barrier_semaphore()

    def greet_seq(i):
        pl.semaphore_signal(
            barrier, inc=1, device_id=(lax.rem(seq + i + 1, S), tp),
            device_id_type=pl.DeviceIdType.MESH,
        )

    def greet_tp(i):
        pl.semaphore_signal(
            barrier, inc=1, device_id=(seq, lax.rem(tp + i + 1, T)),
            device_id_type=pl.DeviceIdType.MESH,
        )

    each(T - 1, greet_tp)
    each(S - 1, greet_seq)

    def piece_rows(c):
        return pl.ds(pl.multiple_of(c * piece, 16), piece)

    def chunk_rows(k):
        return pl.ds(pl.multiple_of(k * chunk, 16), chunk)

    def local(source, target, index):
        return pltpu.make_async_copy(source, target, load_sem.at[index])

    grad_load = local(grad_hbm, grad, 0)
    resid_load = local(resid_hbm, resid, 1)

    def hidden_load(c):
        r = piece_rows(c)
        return (
            pltpu.make_async_copy(clean_hbm.at[r], clean.at[r], piece_sem.at[0, c]),
            pltpu.make_async_copy(corrupt_hbm.at[r], corrupt.at[r], piece_sem.at[1, c]),
        )

    def start_hidden(c):
        for load in hidden_load(c):
            load.start()

    def ids_load(k):
        return local(patched_hbm.at[pl.ds(pl.multiple_of(k * lanes, lanes), lanes)], patched.at[k, 0], 2 + k)

    def weight_load(c):
        return pltpu.make_async_copy(
            weight_hbm.at[piece_rows(c)], weight.at[piece_rows(c)], weight_sem.at[c]
        )

    start_hidden(0)
    grad_load.start()
    each(C - 1, lambda c: start_hidden(c + 1))

    def remote(source, target, send, recv, device):
        return pltpu.make_async_remote_copy(
            src_ref=source, dst_ref=target, send_sem=send, recv_sem=recv,
            device_id=device, device_id_type=pl.DeviceIdType.MESH,
        )

    keep = pl.ds(pl.multiple_of(upper * half, 8), half)
    give = pl.ds(pl.multiple_of((1 - upper) * half, 8), half)

    def grad_copy(k):
        r = chunk_rows(k)
        return remote(
            grad.at[r], partner_grad.at[r], pair_send.at[k], pair_recv.at[k], (partner, tp)
        )

    resid_copy = remote(
        resid.at[give], partner_resid, pair_send.at[K], pair_recv.at[K], (partner, tp)
    )
    score_copy = remote(
        score_out, scored.at[upper], pair_send.at[K + 1], pair_recv.at[K + 1], (partner, tp)
    )

    def diff_copy(block, c, step):
        place = diff.at[block, piece_rows(c)]
        direction = (step + 1) // 2
        return remote(
            place, place, diff_send.at[direction, block, c], diff_recv.at[block, c],
            (seq, tp + step),
        )

    def forward(block, c, step):
        @pl.when((tp + step >= 0) & (tp + step < T))
        def _():
            diff_copy(block, c, step).start()

    def own(c):
        forward(tp, c, 1)
        forward(tp, c, -1)

    def subtract(c):
        for load in hidden_load(c):
            load.wait()
        r = piece_rows(c)
        diff[tp, r, :] = (clean[r, :].astype(F32) - corrupt[r, :].astype(F32)).astype(BF16)
        own(c)

    pl.semaphore_wait(barrier, S - 1 + T - 1)
    subtract(0)
    grad_load.wait()
    each(K, lambda k: grad_copy(k).start())
    each(C - 1, lambda c: subtract(c + 1))
    resid_load.start()
    each(patched.shape[0], lambda k: ids_load(k).start())
    each(C, lambda c: weight_load(c).start())

    def relay(s, c):
        @pl.when(tp - s >= 0)
        def _():
            diff_copy(tp - s, c, 1).wait_recv()
            if s + 1 <= T - 2:
                forward(tp - s, c, 1)

        @pl.when(tp + s < T)
        def _():
            diff_copy(tp + s, c, -1).wait_recv()
            if s + 1 <= T - 2:
                forward(tp + s, c, -1)

    outer = pairs // 2
    mine = lax.rem(seq, pairs)
    chip = mine // 2
    core = lax.rem(mine, 2)

    def mean_copy(block, h, send, target):
        place = means.at[block, chunk_rows(h)]
        return remote(place, place, send, mean_recv.at[block, h], (upper * pairs + target, tp))

    def outer_copy(i, h):
        return mean_copy(mine, h, outer_send.at[i, h], lax.rem(chip + i, outer) * 2 + core)

    def inner_copy(i, h):
        block = lax.rem(chip + i, outer) * 2 + core
        return mean_copy(block, h, inner_send.at[i, h], chip * 2 + 1 - core)

    def await_mean(block, h):
        mean_copy(block, h, inner_send.at[0, h], chip * 2 + 1 - core).wait_recv()

    counts[...] = jnp.zeros_like(counts)
    group_ids = lax.broadcasted_iota(jnp.int32, (G, lanes), 0)
    lane_ids = lax.broadcasted_iota(jnp.int32, (L, lanes), 0)

    def count(k):
        ids = patched[k] - seq * units + S * units
        high = ids // L - (S * units) // L
        low = lax.rem(ids, L)
        counts[...] += lax.dot_general(
            jnp.where(high == group_ids, 1.0, 0.0).astype(BF16),
            jnp.where(low == lane_ids, 1.0, 0.0).astype(BF16),
            NT, preferred_element_type=F32,
        )

    def spread(g):
        row = jnp.broadcast_to(counts[pl.ds(g, 1), :], (128, L))
        mask[pl.ds(pl.multiple_of(g * L, 8), L), :] = row.T

    def average(k):
        grad_copy(k).wait_recv()
        r = chunk_rows(k)
        both = grad[r, :].astype(F32) + partner_grad[r, :].astype(F32)
        means[mine, r, :] = (both * 0.5).astype(BF16)
        each(outer - 1, lambda i: outer_copy(i + 1, k).start())
        inner_copy(0, k).start()

    def pass_on(k):
        def step(i):
            await_mean(lax.rem(chip + i + 1, outer) * 2 + core, k)
            inner_copy(i + 1, k).start()

        each(outer - 1, step)

    each(patched.shape[0], lambda k: ids_load(k).wait())
    average(0)
    each(patched.shape[0] // 2, count)
    average(1)
    each(patched.shape[0] - patched.shape[0] // 2, lambda k: count(k + patched.shape[0] // 2))

    def average_and_pass(k):
        average(k + 2)
        pass_on(k)

    each(K - 2, average_and_pass)
    resid_load.wait()
    resid_copy.start()
    each(G, spread)
    each(C // 2, lambda c: relay(1, c))
    pass_on(K - 2)
    acc[...] = jnp.zeros_like(acc)
    token[...] = jnp.zeros_like(token)
    pass_on(K - 1)

    def await_inner(k):
        each(outer, lambda i: await_mean(lax.rem(chip + i, outer) * 2 + 1 - core, k))

    each(K, await_inner)

    blocks = T // 2
    at_end = (tp == 0) | (tp == T - 1)
    far = jnp.where(tp == 0, T - 1, 0)
    inward = jnp.where(tp == 0, 1, -1)

    def partial_copy(c):
        r = piece_rows(c)
        return remote(
            partial.at[r], partial_in.at[r], part_send.at[c], part_recv.at[c], (seq, tp + inward)
        )

    def multiply(side, c):
        r = piece_rows(c)
        right = means[pl.ds(side * outer, outer)]
        right = right.reshape(outer * rows, right.shape[-1])
        result = lax.dot_general(weight[r, :], right, NT, preferred_element_type=F32)
        for k in range(blocks):
            unit[side * blocks + k, r, :] = result[:, k * local_len : (k + 1) * local_len]

    far_side = 1 - tp // blocks

    def multiply_far(c):
        weight_load(c).wait()
        multiply(far_side, c)

        @pl.when(at_end)
        def _():
            r = piece_rows(c)
            partial[r, :] = unit[far, r, :].astype(BF16)
            partial_copy(c).start()

    each(C // 2, multiply_far)

    def multiply_and_relay(c):
        multiply_far(c + C // 2)
        relay(1, c + C // 2)

    each(C - C // 2, multiply_and_relay)
    each(C, lambda c: multiply(1 - far_side, c))

    def product(block, c):
        r = piece_rows(c)
        value = diff[block, r, :].astype(F32) * unit[block, r, :]
        masks = mask[r, :]
        for k in range(local_len // 128):
            part = value[:, k * 128 : (k + 1) * 128]
            acc[r, :] += part
            token[block, :, k * 128 : (k + 1) * 128] += jnp.sum(
                part * masks, axis=0, keepdims=True
            )

    def products(s, c):
        if s == 0:
            product(tp, c)
            return

        @pl.when(tp - s >= 0)
        def _():
            product(tp - s, c)

        @pl.when(tp + s < T)
        def _():
            product(tp + s, c)

    resid_copy.wait()
    sign = (1 - 2 * upper).astype(F32)

    difference = sign * (resid[keep, :].astype(F32) - partner_resid[...].astype(F32))

    def score(gradient):
        terms = difference * gradient.astype(F32)
        folded = terms[:, 0:128]
        for j in range(1, terms.shape[1] // 128):
            folded = folded + terms[:, j * 128 : (j + 1) * 128]
        return jnp.sum(folded.T, axis=0, keepdims=True)

    score_out[...] = score(partner_grad[keep, :])
    score_copy.start()
    scored[upper] = score(grad[keep, :])
    each(C, lambda c: products(0, c))
    each(C, lambda c: products(1, c))
    helped = ((tp == 1) | (tp == T - 2)) & (T > 2)
    helped_block = jnp.where(tp == 1, T - 1, 0)

    def help_in(c):
        @pl.when(helped)
        def _():
            r = piece_rows(c)
            remote(
                partial.at[r], partial_in.at[r], part_send.at[c], part_recv.at[c],
                (seq, jnp.where(tp == 1, 0, T - 1)),
            ).wait_recv()
            unit[helped_block, r, :] += partial_in[r, :].astype(F32)

    per = G // C
    kept = G - per

    def fold(g, target, row):
        block = acc[pl.ds(pl.multiple_of(g * L, 8), L), :]
        target[pl.ds(row, 1), :] = jnp.sum(block.T, axis=0, keepdims=True)

    score_copy.wait()
    message[kept:, :] = jnp.zeros((2, L), F32)
    for k in range(2):
        message[kept + k : kept + k + 1, 0:half] = scored[k]

    me = seq * T + tp
    late = lax.rem(tp + T // 2, T)

    def token_copy(s, block):
        return remote(
            token.at[block], token_in.at[me], tok_send.at[0], tok_recv.at[0], (s, block)
        )

    each(S - 1, lambda i: token_copy(lax.rem(seq + i + 1, S), tp).start())
    for k in range(1, T):
        if k != T // 2:
            each(S, lambda i: token_copy(lax.rem(seq + i, S), lax.rem(tp + k, T)).start())
    token_in[me] = token[tp]

    def last(c):
        relay(T - 2, c)
        help_in(c)
        products(T - 2, c)

    def last_and_fold(c):
        last(c)
        each(per, lambda g: fold(c * per + g, message, c * per + g))

    each(C - 1, last_and_fold)

    def share(source, target, send, recv, i):
        return remote(source, target.at[tp], send.at[i], recv.at[tp], (seq, lax.rem(tp + i, T)))

    def message_copy(i):
        return share(message, message_in, msg_send, msg_recv, i)

    def ending_copy(i):
        return share(ending, ending_in, end_send, end_recv, i)

    each(T - 1, lambda i: message_copy(i + 1).start())
    last(C - 1)
    each(S, lambda i: token_copy(lax.rem(seq + i, S), late).start())
    for g in range(per):
        fold(kept + g, ending, g)
    each(T - 1, lambda i: ending_copy(i + 1).start())
    message_in[tp] = message[...]
    ending_in[tp] = ending[...]

    def sent_means(k):
        grad_copy(k).wait_send()
        each(outer - 1, lambda i: outer_copy(i + 1, k).wait_send())
        each(outer, lambda i: inner_copy(i, k).wait_send())

    each(K, sent_means)

    def drain(c):
        def sent(block, step):
            @pl.when((tp + step >= 0) & (tp + step < T) & (block >= 0) & (block < T))
            def _():
                diff_copy(block, c, step).wait_send()

        for s in range(T - 2):
            sent(tp - s, 1)
            sent(tp + s, -1)

    each(C, drain)

    @pl.when(at_end)
    def _():
        each(C, lambda c: partial_copy(c).wait_send())

    def await_message(i):
        source = lax.rem(tp + i + 1, T)
        remote(
            message, message_in.at[source], msg_send.at[0], msg_recv.at[source], (seq, source)
        ).wait_recv()

    each(T - 1, await_message)
    total = jnp.sum(message_in[...], axis=0)
    scores[0:kept, :] = total[:kept] * scales[2]
    scores[G : G + 2, :] = total[kept:] * scales[0]

    def await_ending(i):
        source = lax.rem(tp + i + 1, T)
        remote(
            ending, ending_in.at[source], end_send.at[0], end_recv.at[source], (seq, source)
        ).wait_recv()

    each(T - 1, await_ending)
    scores[kept:G, :] = jnp.sum(ending_in[...], axis=0) * scales[2]
    others = token_in.at[pl.ds(0, S * T - 1)]
    tokens = remote(others, others, tok_send.at[0], tok_recv.at[0], (seq, tp))
    tokens.wait_recv()
    token_total = jnp.sum(token_in[...], axis=0) * scales[1]
    for k in range(local_len // L):
        scores[G + 2 + k : G + 3 + k, :] = token_total[:, k * L : (k + 1) * L]

    tokens.wait_send()
    each(T - 1, lambda i: message_copy(i + 1).wait_send())
    each(T - 1, lambda i: ending_copy(i + 1).wait_send())


def write(G, K, L, half, scores, resid_out, token_out, neuron_out):
    for k in range(2):
        resid_out[k * half : (k + 1) * half] = scores[G + k, 0:half]
    for k in range(K):
        token_out[k * L : (k + 1) * L] = scores[G + 2 + k, :]
    for g in range(G):
        neuron_out[g * L : (g + 1) * L] = scores[g, :]


def shards(grad_out, resid_in, down_weight, hidden_clean, hidden_corrupt, patched):
    S = lax.axis_size("seq")
    T = lax.axis_size("tp")
    rows, width = grad_out.shape
    units, local_len = hidden_clean.shape
    L = math.gcd(units, 128)
    G = units // L
    C = max(c for c in range(1, 9) if G % c == 0)
    lanes = math.gcd(patched.shape[0], 1024)
    half = rows // 2
    scales = (
        1.0 / math.sqrt(width * T),
        1.0 / math.sqrt(patched.shape[0]),
        1.0 / math.sqrt(local_len * T),
    )
    dma = lambda *shape: pltpu.SemaphoreType.DMA(shape)
    K = local_len // L
    chunks = rows // 16
    scores = pl.pallas_call(
        functools.partial(kernel, S, T, C, G, L, chunks, scales),
        out_shape=jax.ShapeDtypeStruct((G + 2 + K, L), F32),
        in_specs=[pl.BlockSpec(memory_space=pl.ANY)] * 6,
        out_specs=pl.BlockSpec(memory_space=pltpu.VMEM),
        scratch_shapes=[
            pltpu.VMEM((rows, width), BF16),
            pltpu.VMEM((rows, width), BF16),
            pltpu.VMEM((units, width), BF16),
            pltpu.VMEM((units, local_len), BF16),
            pltpu.VMEM((units, local_len), BF16),
            pltpu.VMEM((patched.shape[0] // lanes, 1, lanes), jnp.int32),
            pltpu.VMEM((rows, width), BF16),
            pltpu.VMEM((half, width), BF16),
            pltpu.VMEM((S // 2, rows, width), BF16),
            pltpu.VMEM((T, units, local_len), BF16),
            pltpu.VMEM((T, units, local_len), F32),
            pltpu.VMEM((units, local_len), BF16),
            pltpu.VMEM((units, local_len), BF16),
            pltpu.VMEM((units, 128), F32),
            pltpu.VMEM((units, 128), F32),
            pltpu.VMEM((T, 1, local_len), F32),
            pltpu.VMEM((S * T, 1, local_len), F32),
            pltpu.VMEM((G - G // C + 2, L), F32),
            pltpu.VMEM((T, G - G // C + 2, L), F32),
            pltpu.VMEM((G // C, L), F32),
            pltpu.VMEM((T, G // C, L), F32),
            pltpu.VMEM((G, L), F32),
            pltpu.VMEM((2, 1, half), F32),
            pltpu.VMEM((1, half), F32),
            dma(2 + patched.shape[0] // lanes), dma(2, C), dma(C), dma(chunks + 2), dma(chunks + 2),
            dma(S // 4, chunks), dma(S // 4, chunks), dma(S // 2, chunks),
            dma(2, T, C), dma(T, C), dma(C), dma(C),
            dma(T), dma(T), dma(T), dma(T), dma(1), dma(1),
        ],
        compiler_params=pltpu.CompilerParams(
            collective_id=0, has_side_effects=True, vmem_limit_bytes=56 * 1024 * 1024
        ),
    )(
        grad_out, resid_in, down_weight, hidden_clean, hidden_corrupt,
        patched,
    )
    return pl.pallas_call(
        functools.partial(write, G, K, L, half),
        out_shape=(
            jax.ShapeDtypeStruct((rows,), F32),
            jax.ShapeDtypeStruct((local_len,), F32),
            jax.ShapeDtypeStruct((units,), F32),
        ),
        in_specs=[pl.BlockSpec(memory_space=pltpu.VMEM)],
        out_specs=[pl.BlockSpec(memory_space=pltpu.VMEM)] * 3,
    )(scores)


def solution(mesh):
    in_specs = (P("seq", "tp"), P("seq", "tp"), P("seq", "tp"), P("seq", "tp"), P("seq", "tp"), P())
    out_specs = (P("seq"), P("tp"), P("seq"))
    return jax.shard_map(shards, mesh=mesh, in_specs=in_specs, out_specs=out_specs, check_vma=False)
```

```python
import functools
import math

import jax
import jax.numpy as jnp
from jax import lax
from jax.experimental import pallas as pl
from jax.experimental.pallas import tpu as pltpu
from jax.sharding import PartitionSpec as P

F32 = jnp.float32
BF16 = jnp.bfloat16
NT = (((1,), (1,)), ((), ()))


def each(count, body):
    def step(index, carry):
        body(index)
        return carry

    lax.fori_loop(0, count, step, 0)


def kernel(
    S, T, C, G, L, K, scales,
    grad_hbm, resid_hbm, weight_hbm, clean_hbm, corrupt_hbm, patched_hbm,
    scores,
    grad, resid, weight, clean, corrupt, patched,
    partner_grad, partner_resid, means, diff, unit, partial, partial_in, mask, acc, token, token_in,
    message, message_in, ending, ending_in, counts, scored, score_out,
    load_sem, piece_sem, weight_sem, pair_send, pair_recv, outer_send, inner_send, mean_recv, diff_send, diff_recv,
    part_send, part_recv, msg_send, msg_recv, end_send, end_recv, tok_send, tok_recv,
):
    assert T == 4
    seq = lax.axis_index("seq")
    tp = lax.axis_index("tp")
    pairs = S // 2
    partner = lax.rem(seq + pairs, S)
    upper = seq // pairs
    rows = grad.shape[0]
    half = rows // 2
    units = weight.shape[0]
    piece = units // C
    local_len = diff.shape[2]

    lanes = patched.shape[2]
    chunk = rows // K
    barrier = pltpu.get_barrier_semaphore()

    outer = pairs // 2
    mine = lax.rem(seq, pairs)
    chip = mine // 2
    core = lax.rem(mine, 2)

    def greet(i, j):
        pl.semaphore_signal(
            barrier, inc=1, device_id=(i, j), device_id_type=pl.DeviceIdType.MESH
        )

    def piece_rows(c):
        return pl.ds(pl.multiple_of(c * piece, 16), piece)

    def chunk_rows(k):
        return pl.ds(pl.multiple_of(k * chunk, 16), chunk)

    def local(source, target, index):
        return pltpu.make_async_copy(source, target, load_sem.at[index])

    grad_load = local(grad_hbm, grad, 0)
    resid_load = local(resid_hbm, resid, 1)

    def hidden_load(c):
        r = piece_rows(c)
        return (
            pltpu.make_async_copy(clean_hbm.at[r], clean.at[r], piece_sem.at[0, c]),
            pltpu.make_async_copy(corrupt_hbm.at[r], corrupt.at[r], piece_sem.at[1, c]),
        )

    def start_hidden(c):
        for load in hidden_load(c):
            load.start()

    def ids_load(k):
        return local(patched_hbm.at[pl.ds(pl.multiple_of(k * lanes, lanes), lanes)], patched.at[k, 0], 2 + k)

    def weight_load(c):
        return pltpu.make_async_copy(
            weight_hbm.at[piece_rows(c)], weight.at[piece_rows(c)], weight_sem.at[c]
        )

    start_hidden(0)
    each(T - 1, lambda i: greet(seq, lax.rem(tp + i + 1, T)))
    greet(partner, tp)
    greet(upper * pairs + chip * 2 + 1 - core, tp)
    each(outer - 1, lambda i: greet(upper * pairs + lax.rem(chip + i + 1, outer) * 2 + core, tp))
    grad_load.start()
    each(C - 1, lambda c: start_hidden(c + 1))

    def remote(source, target, send, recv, device):
        return pltpu.make_async_remote_copy(
            src_ref=source, dst_ref=target, send_sem=send, recv_sem=recv,
            device_id=device, device_id_type=pl.DeviceIdType.MESH,
        )

    keep = pl.ds(pl.multiple_of(upper * half, 8), half)
    give = pl.ds(pl.multiple_of((1 - upper) * half, 8), half)

    def grad_copy(k):
        r = chunk_rows(k)
        return remote(
            grad.at[r], partner_grad.at[r], pair_send.at[k], pair_recv.at[k], (partner, tp)
        )

    resid_copy = remote(
        resid.at[give], partner_resid, pair_send.at[K], pair_recv.at[K], (partner, tp)
    )
    score_copy = remote(
        score_out, scored.at[upper], pair_send.at[K + 1], pair_recv.at[K + 1], (partner, tp)
    )

    def diff_copy(block, c, step):
        place = diff.at[block, piece_rows(c)]
        direction = (step + 1) // 2
        return remote(
            place, place, diff_send.at[direction, block, c], diff_recv.at[block, c],
            (seq, tp + step),
        )

    def forward(block, c, step):
        @pl.when((tp + step >= 0) & (tp + step < T))
        def _():
            diff_copy(block, c, step).start()

    def own(c):
        @pl.when((tp != 1) | (c < C - 1))
        def _():
            forward(tp, c, 1)

        forward(tp, c, -1)

    def subtract(c):
        for load in hidden_load(c):
            load.wait()
        r = piece_rows(c)
        diff[tp, r, :] = (clean[r, :].astype(F32) - corrupt[r, :].astype(F32)).astype(BF16)
        own(c)

    pl.semaphore_wait(barrier, T + outer)
    subtract(0)
    grad_load.wait()
    each(K, lambda k: grad_copy(k).start())
    each(C - 1, lambda c: subtract(c + 1))
    resid_load.start()
    each(patched.shape[0], lambda k: ids_load(k).start())
    each(C, lambda c: weight_load(c).start())

    def relay(c):
        @pl.when((tp >= 1) & ((tp != 2) | (c < C - 1)))
        def _():
            diff_copy(tp - 1, c, 1).wait_recv()

            @pl.when((tp == 2) & (c == C - 2))
            def _():
                diff_copy(0, 0, 1).wait_recv()
                forward(0, 0, 1)

            forward(tp - 1, c, 1)

        @pl.when(tp + 1 < T)
        def _():
            diff_copy(tp + 1, c, -1).wait_recv()

            @pl.when(tp >= 1)
            def _():
                forward(tp + 1, c, -1)

    def await_far(c):
        @pl.when(((tp == 2) & (c > 0)) | ((tp == 3) & (c < C - 2)))
        def _():
            diff_copy(tp - 2, c, 1).wait_recv()

        @pl.when(tp < 2)
        def _():
            diff_copy(tp + 2, c, -1).wait_recv()

    def mean_copy(block, h, send, target):
        place = means.at[block, chunk_rows(h)]
        return remote(place, place, send, mean_recv.at[block, h], (upper * pairs + target, tp))

    def outer_copy(i, h):
        return mean_copy(mine, h, outer_send.at[i, h], lax.rem(chip + i, outer) * 2 + core)

    def inner_copy(i, h):
        block = lax.rem(chip + i, outer) * 2 + core
        return mean_copy(block, h, inner_send.at[i, h], chip * 2 + 1 - core)

    def await_mean(block, h):
        mean_copy(block, h, inner_send.at[0, h], chip * 2 + 1 - core).wait_recv()

    counts[...] = jnp.zeros_like(counts)
    group_ids = lax.broadcasted_iota(jnp.int32, (G, lanes), 0)
    lane_ids = lax.broadcasted_iota(jnp.int32, (L, lanes), 0)

    def count(k):
        ids = patched[k] - seq * units + S * units
        high = ids // L - (S * units) // L
        low = lax.rem(ids, L)
        counts[...] += lax.dot_general(
            jnp.where(high == group_ids, 1.0, 0.0).astype(BF16),
            jnp.where(low == lane_ids, 1.0, 0.0).astype(BF16),
            NT, preferred_element_type=F32,
        )

    def spread(g):
        row = jnp.broadcast_to(counts[pl.ds(g, 1), :], (128, L))
        mask[pl.ds(pl.multiple_of(g * L, 8), L), :] = row.T

    def average(k):
        grad_copy(k).wait_recv()
        r = chunk_rows(k)
        both = grad[r, :].astype(F32) + partner_grad[r, :].astype(F32)
        means[mine, r, :] = (both * 0.5).astype(BF16)
        each(outer - 1, lambda i: outer_copy(i + 1, k).start())
        inner_copy(0, k).start()

    def pass_on(k):
        def step(i):
            await_mean(lax.rem(chip + i + 1, outer) * 2 + core, k)
            inner_copy(i + 1, k).start()

        each(outer - 1, step)

    average(0)
    average(1)

    def average_and_pass(k):
        average(k + 2)
        pass_on(k)

    each(K - 2, average_and_pass)
    resid_load.wait()
    resid_copy.start()
    each(C // 2, relay)
    pass_on(K - 2)
    acc[...] = jnp.zeros_like(acc)
    token[...] = jnp.zeros_like(token)
    pass_on(K - 1)

    def await_inner(k):
        each(outer, lambda i: await_mean(lax.rem(chip + i, outer) * 2 + 1 - core, k))

    each(K, await_inner)

    blocks = T // 2
    at_end = (tp == 0) | (tp == T - 1)
    far = jnp.where(tp == 0, T - 1, 0)
    inward = jnp.where(tp == 0, 1, -1)

    def partial_copy(c):
        r = piece_rows(c)
        return remote(
            partial.at[r], partial_in.at[r], part_send.at[c], part_recv.at[c], (seq, tp + inward)
        )

    def multiply(side, c):
        r = piece_rows(c)
        right = means[pl.ds(side * outer, outer)]
        right = right.reshape(outer * rows, right.shape[-1])
        result = lax.dot_general(weight[r, :], right, NT, preferred_element_type=F32)
        for k in range(blocks):
            unit[side * blocks + k, r, :] = result[:, k * local_len : (k + 1) * local_len]

    far_side = 1 - tp // blocks

    def multiply_far(c):
        weight_load(c).wait()
        multiply(far_side, c)

        def export(block, source, slot):
            partial[piece_rows(slot), :] = unit[block, piece_rows(source), :].astype(BF16)
            partial_copy(slot).start()

        @pl.when((tp == 0) | ((tp == T - 1) & (c > 0)))
        def _():
            export(far, c, c)

        @pl.when((tp == T - 1) & (c == C - 1))
        def _():
            export(1, C - 1, 0)

    each(C // 2, multiply_far)

    def multiply_and_relay(c):
        multiply_far(c + C // 2)
        relay(c + C // 2)

    each(C - C // 2, multiply_and_relay)

    @pl.when(tp == 1)
    def _():
        forward(tp, C - 1, 1)

    each(C, lambda c: multiply(1 - far_side, c))
    each(patched.shape[0], lambda k: ids_load(k).wait())
    each(patched.shape[0], count)
    each(G, spread)

    def product(block, c):
        r = piece_rows(c)
        value = diff[block, r, :].astype(F32) * unit[block, r, :]
        masks = mask[r, :]
        for k in range(local_len // 128):
            part = value[:, k * 128 : (k + 1) * 128]
            acc[r, :] += part
            token[block, :, k * 128 : (k + 1) * 128] += jnp.sum(
                part * masks, axis=0, keepdims=True
            )

    def products(s, c):
        if s == 0:
            product(tp, c)
            return

        if s == 1:
            left = (tp >= 1) & ((tp != 2) | (c < C - 1))
        else:
            left = (tp == 2) | ((tp == 3) & (c < C - 2))

        @pl.when(left)
        def _():
            product(tp - s, c)

        @pl.when(tp + s < T)
        def _():
            product(tp + s, c)

    resid_copy.wait()
    sign = (1 - 2 * upper).astype(F32)

    difference = sign * (resid[keep, :].astype(F32) - partner_resid[...].astype(F32))

    def score(gradient):
        terms = difference * gradient.astype(F32)
        folded = terms[:, 0:128]
        for j in range(1, terms.shape[1] // 128):
            folded = folded + terms[:, j * 128 : (j + 1) * 128]
        return jnp.sum(folded.T, axis=0, keepdims=True)

    score_out[...] = score(partner_grad[keep, :])
    score_copy.start()
    scored[upper] = score(grad[keep, :])
    each(C, lambda c: products(0, c))
    each(C, lambda c: products(1, c))
    def help_with(block, target, slot):
        part = piece_rows(slot)
        remote(
            partial.at[part], partial_in.at[part], part_send.at[slot], part_recv.at[slot],
            (seq, jnp.where(tp == 1, 0, T - 1)),
        ).wait_recv()
        unit[block, piece_rows(target), :] += partial_in[part, :].astype(F32)

    def help_in(c):
        @pl.when((tp == 1) | ((tp == 2) & (c > 0)))
        def _():
            help_with(jnp.where(tp == 1, T - 1, 0), c, c)

    per = G // C
    kept = G - per

    def fold(g, target, row):
        block = acc[pl.ds(pl.multiple_of(g * L, 8), L), :]
        target[pl.ds(row, 1), :] = jnp.sum(block.T, axis=0, keepdims=True)

    score_copy.wait()
    message[kept:, :] = jnp.zeros((2, L), F32)
    for k in range(2):
        message[kept + k : kept + k + 1, 0:half] = scored[k]

    me = seq * T + tp
    other = jnp.where(tp == 3, 2, tp + 1)
    middle = jnp.where(tp == 0, 3, 0)
    late = jnp.where(tp < 2, tp + 2, 1)

    def token_copy(s, block):
        return remote(
            token.at[block], token_in.at[me], tok_send.at[0], tok_recv.at[0], (s, block)
        )

    def send_tokens(block):
        each(S, lambda i: token_copy(lax.rem(seq + i, S), block).start())

    each(S - 1, lambda i: token_copy(lax.rem(seq + i + 1, S), tp).start())
    send_tokens(other)

    @pl.when(tp < 2)
    def _():
        send_tokens(middle)

    token_in[me] = token[tp]

    def last(c):
        await_far(c)
        help_in(c)
        products(2, c)

    def last_and_fold(c):
        last(c)
        each(per, lambda g: fold(c * per + g, message, c * per + g))

    def sent_means(k):
        grad_copy(k).wait_send()
        each(outer - 1, lambda i: outer_copy(i + 1, k).wait_send())
        each(outer, lambda i: inner_copy(i, k).wait_send())

    def drain_own(c):
        @pl.when((tp < T - 1) & ((tp != 1) | (c < C - 1)))
        def _():
            diff_copy(tp, c, 1).wait_send()

        @pl.when(tp > 0)
        def _():
            diff_copy(tp, c, -1).wait_send()

    def drain_relay(c):
        @pl.when((tp == 1) | ((tp == 2) & (c < C - 1)))
        def _():
            diff_copy(tp - 1, c, 1).wait_send()

        @pl.when((tp == 1) | (tp == 2))
        def _():
            diff_copy(tp + 1, c, -1).wait_send()

    each(K, sent_means)
    each(C, drain_own)
    each(C - 1, last_and_fold)

    def share(source, target, send, recv, i):
        return remote(source, target.at[tp], send.at[i], recv.at[tp], (seq, lax.rem(tp + i, T)))

    def message_copy(i):
        return share(message, message_in, msg_send, msg_recv, i)

    def ending_copy(i):
        return share(ending, ending_in, end_send, end_recv, i)

    def send_message():
        each(T - 1, lambda i: message_copy(i + 1).start())

    @pl.when(tp < 3)
    def _():
        send_message()

    def send_ending():
        for g in range(per):
            fold(kept + g, ending, g)
        each(T - 1, lambda i: ending_copy(i + 1).start())

    def refold(c):
        for g in range(per):
            fold(c * per + g, message, c * per + g)

    last(C - 1)

    @pl.when(tp == 2)
    def _():
        send_tokens(0)
        diff_copy(1, C - 1, 1).wait_recv()
        help_with(1, C - 1, 0)
        product(1, C - 1)

    @pl.when(tp == 3)
    def _():
        diff_copy(0, 0, 1).wait_recv()
        product(0, 0)
        send_tokens(0)
        refold(0)
        send_ending()
        diff_copy(1, C - 2, 1).wait_recv()
        product(1, C - 2)

    send_tokens(late)

    @pl.when(tp < 3)
    def _():
        send_ending()

    @pl.when(tp == 3)
    def _():
        refold(C - 2)
        send_message()

    message_in[tp] = message[...]
    ending_in[tp] = ending[...]

    @pl.when(at_end)
    def _():
        each(C, lambda c: partial_copy(c).wait_send())

    each(C, drain_relay)

    @pl.when(tp == 1)
    def _():
        diff_copy(1, C - 1, 1).wait_send()

    @pl.when(tp == 2)
    def _():
        diff_copy(0, 0, 1).wait_send()

    def await_message(i):
        source = lax.rem(tp + i + 1, T)
        remote(
            message, message_in.at[source], msg_send.at[0], msg_recv.at[source], (seq, source)
        ).wait_recv()

    each(T - 1, await_message)
    total = jnp.sum(message_in[...], axis=0)
    scores[0:kept, :] = total[:kept] * scales[2]
    scores[G : G + 2, :] = total[kept:] * scales[0]

    each(T - 1, lambda i: message_copy(i + 1).wait_send())

    def await_ending(i):
        source = lax.rem(tp + i + 1, T)
        remote(
            ending, ending_in.at[source], end_send.at[0], end_recv.at[source], (seq, source)
        ).wait_recv()

    each(T - 1, await_ending)
    scores[kept:G, :] = jnp.sum(ending_in[...], axis=0) * scales[2]
    others = token_in.at[pl.ds(0, S * T - 1)]
    tokens = remote(others, others, tok_send.at[0], tok_recv.at[0], (seq, tp))
    tokens.wait_recv()
    token_total = jnp.sum(token_in[...], axis=0) * scales[1]
    for k in range(local_len // L):
        scores[G + 2 + k : G + 3 + k, :] = token_total[:, k * L : (k + 1) * L]

    tokens.wait_send()
    each(T - 1, lambda i: ending_copy(i + 1).wait_send())


def write(G, K, L, half, scores, resid_out, token_out, neuron_out):
    for k in range(2):
        resid_out[k * half : (k + 1) * half] = scores[G + k, 0:half]
    for k in range(K):
        token_out[k * L : (k + 1) * L] = scores[G + 2 + k, :]
    for g in range(G):
        neuron_out[g * L : (g + 1) * L] = scores[g, :]


def shards(grad_out, resid_in, down_weight, hidden_clean, hidden_corrupt, patched):
    S = lax.axis_size("seq")
    T = lax.axis_size("tp")
    rows, width = grad_out.shape
    units, local_len = hidden_clean.shape
    L = math.gcd(units, 128)
    G = units // L
    C = max(c for c in range(1, 9) if G % c == 0)
    lanes = math.gcd(patched.shape[0], 1024)
    half = rows // 2
    scales = (
        1.0 / math.sqrt(width * T),
        1.0 / math.sqrt(patched.shape[0]),
        1.0 / math.sqrt(local_len * T),
    )
    dma = lambda *shape: pltpu.SemaphoreType.DMA(shape)
    K = local_len // L
    chunks = rows // 16
    scores = pl.pallas_call(
        functools.partial(kernel, S, T, C, G, L, chunks, scales),
        out_shape=pltpu.VMEM((G + 2 + K, L), F32),
        in_specs=[pl.BlockSpec(memory_space=pl.ANY)] * 6,
        out_specs=pl.BlockSpec(memory_space=pltpu.VMEM),
        scratch_shapes=[
            pltpu.VMEM((rows, width), BF16),
            pltpu.VMEM((rows, width), BF16),
            pltpu.VMEM((units, width), BF16),
            pltpu.VMEM((units, local_len), BF16),
            pltpu.VMEM((units, local_len), BF16),
            pltpu.VMEM((patched.shape[0] // lanes, 1, lanes), jnp.int32),
            pltpu.VMEM((rows, width), BF16),
            pltpu.VMEM((half, width), BF16),
            pltpu.VMEM((S // 2, rows, width), BF16),
            pltpu.VMEM((T, units, local_len), BF16),
            pltpu.VMEM((T, units, local_len), F32),
            pltpu.VMEM((units, local_len), BF16),
            pltpu.VMEM((units, local_len), BF16),
            pltpu.VMEM((units, 128), F32),
            pltpu.VMEM((units, 128), F32),
            pltpu.VMEM((T, 1, local_len), F32),
            pltpu.VMEM((S * T, 1, local_len), F32),
            pltpu.VMEM((G - G // C + 2, L), F32),
            pltpu.VMEM((T, G - G // C + 2, L), F32),
            pltpu.VMEM((G // C, L), F32),
            pltpu.VMEM((T, G // C, L), F32),
            pltpu.VMEM((G, L), F32),
            pltpu.VMEM((2, 1, half), F32),
            pltpu.VMEM((1, half), F32),
            dma(2 + patched.shape[0] // lanes), dma(2, C), dma(C), dma(chunks + 2), dma(chunks + 2),
            dma(S // 4, chunks), dma(S // 4, chunks), dma(S // 2, chunks),
            dma(2, T, C), dma(T, C), dma(C), dma(C),
            dma(T), dma(T), dma(T), dma(T), dma(1), dma(1),
        ],
        compiler_params=pltpu.CompilerParams(
            collective_id=0, has_side_effects=True, vmem_limit_bytes=56 * 1024 * 1024
        ),
    )(
        grad_out, resid_in, down_weight, hidden_clean, hidden_corrupt,
        patched,
    )
    return pl.pallas_call(
        functools.partial(write, G, K, L, half),
        out_shape=(
            jax.ShapeDtypeStruct((rows,), F32),
            jax.ShapeDtypeStruct((local_len,), F32),
            jax.ShapeDtypeStruct((units,), F32),
        ),
        in_specs=[pl.BlockSpec(memory_space=pltpu.VMEM)],
        out_specs=[pl.BlockSpec(memory_space=pltpu.VMEM)] * 3,
    )(pltpu.with_memory_space_constraint(scores, pltpu.VMEM))


def solution(mesh):
    in_specs = (P("seq", "tp"), P("seq", "tp"), P("seq", "tp"), P("seq", "tp"), P("seq", "tp"), P())
    out_specs = (P("seq"), P("tp"), P("seq"))
    return jax.shard_map(shards, mesh=mesh, in_specs=in_specs, out_specs=out_specs, check_vma=False)
```

```python
import functools
import math

import jax
import jax.numpy as jnp
from jax import lax
from jax.experimental import pallas as pl
from jax.experimental.pallas import tpu as pltpu
from jax.sharding import PartitionSpec as P

F32 = jnp.float32
BF16 = jnp.bfloat16
NT = (((1,), (1,)), ((), ()))


def each(count, body):
    def step(index, carry):
        body(index)
        return carry

    lax.fori_loop(0, count, step, 0)


def kernel(
    S, T, C, G, L, K, scales,
    grad_hbm, resid_hbm, weight_hbm, clean_hbm, corrupt_hbm, patched_hbm,
    scores,
    grad, resid, weight, clean, corrupt, patched,
    partner_grad, partner_resid, means, diff, unit, partial, partial_in, mask, acc, token, token_in,
    message, message_in, ending, ending_in, counts, scored, score_out,
    load_sem, piece_sem, weight_sem, pair_send, pair_recv, outer_send, inner_send, mean_recv, diff_send, diff_recv,
    part_send, part_recv, msg_send, msg_recv, end_send, end_recv, tok_send, tok_recv,
    turn,
):
    assert T == 4
    seq = lax.axis_index("seq")
    tp = lax.axis_index("tp")
    pairs = S // 2
    partner = lax.rem(seq + pairs, S)
    upper = seq // pairs
    rows = grad.shape[0]
    half = rows // 2
    units = weight.shape[0]
    piece = units // C
    local_len = diff.shape[2]
    assert C <= K

    lanes = patched.shape[2]
    chunk = rows // K
    barrier = pltpu.get_barrier_semaphore()

    outer = pairs // 2
    mine = lax.rem(seq, pairs)
    chip = mine // 2
    core = lax.rem(mine, 2)

    sibling = upper * pairs + chip * 2 + 1 - core
    at_end = (tp == 0) | (tp == T - 1)
    single = local_len == rows
    first = core
    if single:
        first = jnp.where(tp == 0, 1, jnp.where(tp == T - 1, 0, core))
    leads = at_end & (core == first) & single
    follows = at_end & (core != first)

    def greet(i, j):
        pl.semaphore_signal(
            barrier, inc=1, device_id=(i, j), device_id_type=pl.DeviceIdType.MESH
        )

    def piece_rows(c):
        return pl.ds(pl.multiple_of(c * piece, 16), piece)

    def chunk_rows(k):
        return pl.ds(pl.multiple_of(k * chunk, 16), chunk)

    def local(source, target, index):
        return pltpu.make_async_copy(source, target, load_sem.at[index])

    grad_load = local(grad_hbm, grad, 0)
    resid_load = local(resid_hbm, resid, 1)

    def hidden_load(c):
        r = piece_rows(c)
        return (
            pltpu.make_async_copy(clean_hbm.at[r], clean.at[r], piece_sem.at[0, c]),
            pltpu.make_async_copy(corrupt_hbm.at[r], corrupt.at[r], piece_sem.at[1, c]),
        )

    def start_hidden(c):
        for load in hidden_load(c):
            load.start()

    def ids_load(k):
        return local(patched_hbm.at[pl.ds(pl.multiple_of(k * lanes, lanes), lanes)], patched.at[k, 0], 2 + k)

    def weight_load(c):
        return pltpu.make_async_copy(
            weight_hbm.at[piece_rows(c)], weight.at[piece_rows(c)], weight_sem.at[c]
        )

    start_hidden(0)
    each(T - 1, lambda i: greet(seq, lax.rem(tp + i + 1, T)))
    greet(partner, tp)
    greet(sibling, tp)
    each(outer - 1, lambda i: greet(upper * pairs + lax.rem(chip + i + 1, outer) * 2 + core, tp))
    grad_load.start()
    each(C - 1, lambda c: start_hidden(c + 1))
    each(patched.shape[0], lambda k: ids_load(k).start())

    def remote(source, target, send, recv, device):
        return pltpu.make_async_remote_copy(
            src_ref=source, dst_ref=target, send_sem=send, recv_sem=recv,
            device_id=device, device_id_type=pl.DeviceIdType.MESH,
        )

    keep = pl.ds(pl.multiple_of(upper * half, 8), half)
    give = pl.ds(pl.multiple_of((1 - upper) * half, 8), half)

    def grad_copy(k):
        r = chunk_rows(k)
        return remote(
            grad.at[r], partner_grad.at[r], pair_send.at[k], pair_recv.at[k], (partner, tp)
        )

    resid_copy = remote(
        resid.at[give], partner_resid, pair_send.at[K], pair_recv.at[K], (partner, tp)
    )
    score_copy = remote(
        score_out, scored.at[upper], pair_send.at[K + 1], pair_recv.at[K + 1], (partner, tp)
    )

    def diff_copy(block, c, step):
        place = diff.at[block, piece_rows(c)]
        direction = (step + 1) // 2
        return remote(
            place, place, diff_send.at[direction, block, c], diff_recv.at[block, c],
            (seq, tp + step),
        )

    def forward(block, c, step):
        @pl.when((tp + step >= 0) & (tp + step < T))
        def _():
            diff_copy(block, c, step).start()

    def own(c):
        @pl.when((tp != 1) | (c < C - 1))
        def _():
            forward(tp, c, 1)

        forward(tp, c, -1)

    def subtract(c):
        for load in hidden_load(c):
            load.wait()
        r = piece_rows(c)
        diff[tp, r, :] = (clean[r, :].astype(F32) - corrupt[r, :].astype(F32)).astype(BF16)
        own(c)

    pl.semaphore_wait(barrier, T + outer)
    subtract(0)
    grad_load.wait()

    @pl.when(~follows)
    def _():
        each(K, lambda k: grad_copy(k).start())

    each(C - 1, lambda c: subtract(c + 1))

    resid_load.start()
    each(C, lambda c: weight_load(c).start())

    def relay(c):
        @pl.when((tp >= 1) & ((tp != 2) | (c < C - 1)))
        def _():
            diff_copy(tp - 1, c, 1).wait_recv()

            @pl.when((tp == 2) & (c == C - 2))
            def _():
                diff_copy(0, 0, 1).wait_recv()
                forward(0, 0, 1)

            forward(tp - 1, c, 1)

        @pl.when(tp + 1 < T)
        def _():
            diff_copy(tp + 1, c, -1).wait_recv()

            @pl.when(tp >= 1)
            def _():
                forward(tp + 1, c, -1)

    def await_far(c):
        @pl.when(((tp == 2) & (c > 0)) | ((tp == 3) & (c < C - 2)))
        def _():
            diff_copy(tp - 2, c, 1).wait_recv()

        @pl.when(tp < 2)
        def _():
            diff_copy(tp + 2, c, -1).wait_recv()

    def mean_copy(block, h, send, target):
        place = means.at[lax.rem(block, 2) * outer + block // 2, chunk_rows(h)]
        return remote(place, place, send, mean_recv.at[block, h], (upper * pairs + target, tp))

    def outer_copy(i, h):
        return mean_copy(mine, h, outer_send.at[i, h], lax.rem(chip + i, outer) * 2 + core)

    def inner_copy(i, h):
        block = lax.rem(chip + i, outer) * 2 + core
        return mean_copy(block, h, inner_send.at[i, h], chip * 2 + 1 - core)

    def await_mean(block, h):
        mean_copy(block, h, inner_send.at[0, h], chip * 2 + 1 - core).wait_recv()

    counts[...] = jnp.zeros_like(counts)
    group_ids = lax.broadcasted_iota(jnp.int32, (G, lanes), 0)
    lane_ids = lax.broadcasted_iota(jnp.int32, (L, lanes), 0)

    def count(k):
        ids = patched[k] - seq * units + S * units
        high = ids // L - (S * units) // L
        low = lax.rem(ids, L)
        counts[...] += lax.dot_general(
            jnp.where(high == group_ids, 1.0, 0.0).astype(BF16),
            jnp.where(low == lane_ids, 1.0, 0.0).astype(BF16),
            NT, preferred_element_type=F32,
        )

    def spread(g):
        row = jnp.broadcast_to(counts[pl.ds(g, 1), :], (128, L))
        mask[pl.ds(pl.multiple_of(g * L, 8), L), :] = row.T

    def average(k):
        grad_copy(k).wait_recv()
        r = chunk_rows(k)
        both = grad[r, :].astype(F32) + partner_grad[r, :].astype(F32)
        means[core * outer + chip, r, :] = (both * 0.5).astype(BF16)
        each(outer - 1, lambda i: outer_copy(i + 1, k).start())
        inner_copy(0, k).start()

        @pl.when(leads & (k == 2))
        def _():
            pl.semaphore_signal(
                turn, inc=1, device_id=(sibling, tp), device_id_type=pl.DeviceIdType.MESH
            )

    def pass_on(k):
        def step(i):
            await_mean(lax.rem(chip + i + 1, outer) * 2 + core, k)
            inner_copy(i + 1, k).start()

        each(outer - 1, step)

    ids = patched.shape[0]
    ahead = max(ids - K, 0)
    each(ids, lambda k: ids_load(k).wait())
    each(ahead, count)

    @pl.when(follows)
    def _():
        pl.semaphore_wait(turn, 1)
        each(K, lambda k: grad_copy(k).start())

    def count_beside(k):
        @pl.when(ahead + k < ids)
        def _():
            count(ahead + k)

    for k in range(2):
        average(k)
        count_beside(k)

    def average_and_pass(k):
        average(k + 2)

        @pl.when(~follows)
        def _():
            pass_on(k)

        count_beside(k + 2)

    each(K - 2, average_and_pass)
    resid_load.wait()
    resid_copy.start()
    each(C // 2, relay)
    each(G, spread)
    acc[...] = jnp.zeros_like(acc)
    token[...] = jnp.zeros_like(token)

    def await_inner(k):
        each(outer, lambda i: await_mean(lax.rem(chip + i, outer) * 2 + 1 - core, k))

    @pl.when(~follows)
    def _():
        pass_on(K - 2)
        pass_on(K - 1)

    @pl.when(follows)
    def _():
        each(K, await_inner)

    far = jnp.where(tp == 0, T - 1, 0)
    inward = jnp.where(tp == 0, 1, -1)

    def partial_copy(c):
        r = piece_rows(c)
        return remote(
            partial.at[r], partial_in.at[r], part_send.at[c], part_recv.at[c], (seq, tp + inward)
        )

    def multiply(side, c):
        r = piece_rows(c)
        right = means[pl.ds(side * outer, outer)]
        right = right.reshape(outer * rows, right.shape[-1])
        result = lax.dot_general(weight[r, :], right, NT, preferred_element_type=F32)
        for j in range(outer):
            part = result[:, j * rows : (j + 1) * rows]
            if single:
                unit[2 * j + side, r, :] = part
            else:
                place = (2 * j + side) * rows
                columns = pl.ds(pl.multiple_of(lax.rem(place, local_len), 128), rows)
                unit[place // local_len, r, columns] = part

    def export(block, source, slot):
        partial[piece_rows(slot), :] = unit[block, piece_rows(source), :].astype(BF16)
        partial_copy(slot).start()

    def ship(c):
        @pl.when((tp == 0) | ((tp == T - 1) & (c > 0)))
        def _():
            export(far, c, c)

    def multiply_first(c):
        weight_load(c).wait()
        multiply(first, c)
        if single:
            ship(c)

        @pl.when(follows)
        def _():
            pass_on(c)

    each(C // 2, multiply_first)

    def multiply_and_relay(c):
        multiply_first(c + C // 2)
        relay(c + C // 2)

    each(C - C // 2, multiply_and_relay)

    @pl.when(tp == 1)
    def _():
        forward(tp, C - 1, 1)

    @pl.when(follows)
    def _():
        each(K - C, lambda k: pass_on(k + C))

    @pl.when(~follows)
    def _():
        each(K, await_inner)

    def multiply_second(c):
        multiply(1 - first, c)
        if not single:
            ship(c)

        @pl.when((tp == T - 1) & (c == C - 1))
        def _():
            export(1, C - 1, 0)

    each(C, multiply_second)

    def product(block, c):
        r = piece_rows(c)
        value = diff[block, r, :].astype(F32) * unit[block, r, :]
        masks = mask[r, :]
        for k in range(local_len // 128):
            part = value[:, k * 128 : (k + 1) * 128]
            acc[r, :] += part
            token[block, :, k * 128 : (k + 1) * 128] += jnp.sum(
                part * masks, axis=0, keepdims=True
            )

    def products(s, c):
        if s == 0:
            product(tp, c)
            return

        if s == 1:
            left = (tp >= 1) & ((tp != 2) | (c < C - 1))
        else:
            left = (tp == 2) | ((tp == 3) & (c < C - 2))

        @pl.when(left)
        def _():
            product(tp - s, c)

        @pl.when(tp + s < T)
        def _():
            product(tp + s, c)

    resid_copy.wait()
    sign = (1 - 2 * upper).astype(F32)

    difference = sign * (resid[keep, :].astype(F32) - partner_resid[...].astype(F32))

    def score(gradient):
        terms = difference * gradient.astype(F32)
        folded = terms[:, 0:128]
        for j in range(1, terms.shape[1] // 128):
            folded = folded + terms[:, j * 128 : (j + 1) * 128]
        return jnp.sum(folded.T, axis=0, keepdims=True)

    score_out[...] = score(partner_grad[keep, :])
    score_copy.start()
    scored[upper] = score(grad[keep, :])
    each(C, lambda c: products(0, c))
    each(C, lambda c: products(1, c))
    def help_with(block, target, slot):
        part = piece_rows(slot)
        remote(
            partial.at[part], partial_in.at[part], part_send.at[slot], part_recv.at[slot],
            (seq, jnp.where(tp == 1, 0, T - 1)),
        ).wait_recv()
        unit[block, piece_rows(target), :] += partial_in[part, :].astype(F32)

    def help_in(c):
        @pl.when((tp == 1) | ((tp == 2) & (c > 0)))
        def _():
            help_with(jnp.where(tp == 1, T - 1, 0), c, c)

    per = G // C
    kept = G - per

    def fold(g, target, row):
        block = acc[pl.ds(pl.multiple_of(g * L, 8), L), :]
        target[pl.ds(row, 1), :] = jnp.sum(block.T, axis=0, keepdims=True)

    score_copy.wait()
    message[kept:, :] = jnp.zeros((2, L), F32)
    for k in range(2):
        message[kept + k : kept + k + 1, 0:half] = scored[k]

    me = seq * T + tp
    other = jnp.where(tp == 3, 2, tp + 1)
    middle = jnp.where(tp == 0, 3, 0)
    late = jnp.where(tp < 2, tp + 2, 1)

    def token_copy(s, block):
        return remote(
            token.at[block], token_in.at[me], tok_send.at[0], tok_recv.at[0], (s, block)
        )

    def send_tokens(block):
        each(S, lambda i: token_copy(lax.rem(seq + i, S), block).start())

    each(S - 1, lambda i: token_copy(lax.rem(seq + i + 1, S), tp).start())
    send_tokens(other)

    @pl.when(tp < 2)
    def _():
        send_tokens(middle)

    token_in[me] = token[tp]

    def last(c):
        await_far(c)
        help_in(c)
        products(2, c)

    def last_and_fold(c):
        last(c)
        each(per, lambda g: fold(c * per + g, message, c * per + g))

    def sent_means(k):
        grad_copy(k).wait_send()
        each(outer - 1, lambda i: outer_copy(i + 1, k).wait_send())
        each(outer, lambda i: inner_copy(i, k).wait_send())

    def drain_own(c):
        @pl.when((tp < T - 1) & ((tp != 1) | (c < C - 1)))
        def _():
            diff_copy(tp, c, 1).wait_send()

        @pl.when(tp > 0)
        def _():
            diff_copy(tp, c, -1).wait_send()

    def drain_relay(c):
        @pl.when((tp == 1) | ((tp == 2) & (c < C - 1)))
        def _():
            diff_copy(tp - 1, c, 1).wait_send()

        @pl.when((tp == 1) | (tp == 2))
        def _():
            diff_copy(tp + 1, c, -1).wait_send()

    each(K, sent_means)
    each(C, drain_own)
    each(C - 1, last_and_fold)

    def share(source, target, send, recv, i):
        return remote(source, target.at[tp], send.at[i], recv.at[tp], (seq, lax.rem(tp + i, T)))

    def message_copy(i):
        return share(message, message_in, msg_send, msg_recv, i)

    def ending_copy(i):
        return share(ending, ending_in, end_send, end_recv, i)

    def send_message():
        each(T - 1, lambda i: message_copy(i + 1).start())

    @pl.when(tp < 3)
    def _():
        send_message()

    def send_ending():
        for g in range(per):
            fold(kept + g, ending, g)
        each(T - 1, lambda i: ending_copy(i + 1).start())

    def refold(c):
        for g in range(per):
            fold(c * per + g, message, c * per + g)

    last(C - 1)

    @pl.when(tp == 2)
    def _():
        send_tokens(0)
        diff_copy(1, C - 1, 1).wait_recv()
        help_with(1, C - 1, 0)
        product(1, C - 1)

    @pl.when(tp == 3)
    def _():
        diff_copy(0, 0, 1).wait_recv()
        product(0, 0)
        send_tokens(0)
        refold(0)
        send_ending()
        diff_copy(1, C - 2, 1).wait_recv()
        product(1, C - 2)

    @pl.when(tp < 3)
    def _():
        send_ending()

    @pl.when(tp == 3)
    def _():
        refold(C - 2)
        send_message()

    send_tokens(late)
    message_in[tp] = message[...]
    ending_in[tp] = ending[...]

    @pl.when(at_end)
    def _():
        each(C, lambda c: partial_copy(c).wait_send())

    each(C, drain_relay)

    @pl.when(tp == 1)
    def _():
        diff_copy(1, C - 1, 1).wait_send()

    @pl.when(tp == 2)
    def _():
        diff_copy(0, 0, 1).wait_send()

    def await_message(i):
        source = lax.rem(tp + i + 1, T)
        remote(
            message, message_in.at[source], msg_send.at[0], msg_recv.at[source], (seq, source)
        ).wait_recv()

    each(T - 1, await_message)
    total = jnp.sum(message_in[...], axis=0)
    scores[0:kept, :] = total[:kept] * scales[2]
    scores[G : G + 2, :] = total[kept:] * scales[0]

    each(T - 1, lambda i: message_copy(i + 1).wait_send())

    def await_ending(i):
        source = lax.rem(tp + i + 1, T)
        remote(
            ending, ending_in.at[source], end_send.at[0], end_recv.at[source], (seq, source)
        ).wait_recv()

    each(T - 1, await_ending)
    scores[kept:G, :] = jnp.sum(ending_in[...], axis=0) * scales[2]
    others = token_in.at[pl.ds(0, S * T - 1)]
    tokens = remote(others, others, tok_send.at[0], tok_recv.at[0], (seq, tp))
    tokens.wait_recv()
    token_total = jnp.sum(token_in[...], axis=0) * scales[1]
    for k in range(local_len // L):
        scores[G + 2 + k : G + 3 + k, :] = token_total[:, k * L : (k + 1) * L]

    tokens.wait_send()
    each(T - 1, lambda i: ending_copy(i + 1).wait_send())


def write(G, K, L, half, scores, resid_out, token_out, neuron_out):
    for k in range(2):
        resid_out[k * half : (k + 1) * half] = scores[G + k, 0:half]
    for k in range(K):
        token_out[k * L : (k + 1) * L] = scores[G + 2 + k, :]
    for g in range(G):
        neuron_out[g * L : (g + 1) * L] = scores[g, :]


def shards(grad_out, resid_in, down_weight, hidden_clean, hidden_corrupt, patched):
    S = lax.axis_size("seq")
    T = lax.axis_size("tp")
    rows, width = grad_out.shape
    units, local_len = hidden_clean.shape
    L = math.gcd(units, 128)
    G = units // L
    C = max(c for c in range(1, 9) if G % c == 0)
    lanes = math.gcd(patched.shape[0], 1024)
    half = rows // 2
    scales = (
        1.0 / math.sqrt(width * T),
        1.0 / math.sqrt(patched.shape[0]),
        1.0 / math.sqrt(local_len * T),
    )
    dma = lambda *shape: pltpu.SemaphoreType.DMA(shape)
    K = local_len // L
    chunks = rows // 16
    scores = pl.pallas_call(
        functools.partial(kernel, S, T, C, G, L, chunks, scales),
        out_shape=pltpu.VMEM((G + 2 + K, L), F32),
        in_specs=[pl.BlockSpec(memory_space=pl.ANY)] * 6,
        out_specs=pl.BlockSpec(memory_space=pltpu.VMEM),
        scratch_shapes=[
            pltpu.VMEM((rows, width), BF16),
            pltpu.VMEM((rows, width), BF16),
            pltpu.VMEM((units, width), BF16),
            pltpu.VMEM((units, local_len), BF16),
            pltpu.VMEM((units, local_len), BF16),
            pltpu.VMEM((patched.shape[0] // lanes, 1, lanes), jnp.int32),
            pltpu.VMEM((rows, width), BF16),
            pltpu.VMEM((half, width), BF16),
            pltpu.VMEM((S // 2, rows, width), BF16),
            pltpu.VMEM((T, units, local_len), BF16),
            pltpu.VMEM((T, units, local_len), F32),
            pltpu.VMEM((units, local_len), BF16),
            pltpu.VMEM((units, local_len), BF16),
            pltpu.VMEM((units, 128), F32),
            pltpu.VMEM((units, 128), F32),
            pltpu.VMEM((T, 1, local_len), F32),
            pltpu.VMEM((S * T, 1, local_len), F32),
            pltpu.VMEM((G - G // C + 2, L), F32),
            pltpu.VMEM((T, G - G // C + 2, L), F32),
            pltpu.VMEM((G // C, L), F32),
            pltpu.VMEM((T, G // C, L), F32),
            pltpu.VMEM((G, L), F32),
            pltpu.VMEM((2, 1, half), F32),
            pltpu.VMEM((1, half), F32),
            dma(2 + patched.shape[0] // lanes), dma(2, C), dma(C), dma(chunks + 2), dma(chunks + 2),
            dma(S // 4, chunks), dma(S // 4, chunks), dma(S // 2, chunks),
            dma(2, T, C), dma(T, C), dma(C), dma(C),
            dma(T), dma(T), dma(T), dma(T), dma(1), dma(1),
            pltpu.SemaphoreType.REGULAR,
        ],
        compiler_params=pltpu.CompilerParams(
            collective_id=0, has_side_effects=True, vmem_limit_bytes=56 * 1024 * 1024
        ),
    )(
        grad_out, resid_in, down_weight, hidden_clean, hidden_corrupt,
        patched,
    )
    return pl.pallas_call(
        functools.partial(write, G, K, L, half),
        out_shape=(
            jax.ShapeDtypeStruct((rows,), F32),
            jax.ShapeDtypeStruct((local_len,), F32),
            jax.ShapeDtypeStruct((units,), F32),
        ),
        in_specs=[pl.BlockSpec(memory_space=pltpu.VMEM)],
        out_specs=[pl.BlockSpec(memory_space=pltpu.VMEM)] * 3,
    )(pltpu.with_memory_space_constraint(scores, pltpu.VMEM))


def solution(mesh):
    in_specs = (P("seq", "tp"), P("seq", "tp"), P("seq", "tp"), P("seq", "tp"), P("seq", "tp"), P())
    out_specs = (P("seq"), P("tp"), P("seq"))
    return jax.shard_map(shards, mesh=mesh, in_specs=in_specs, out_specs=out_specs, check_vma=False)
```

```python
import functools
import math

import jax
import jax.numpy as jnp
from jax import lax
from jax.experimental import pallas as pl
from jax.experimental.pallas import tpu as pltpu
from jax.sharding import PartitionSpec as P

F32 = jnp.float32
BF16 = jnp.bfloat16
NT = (((1,), (1,)), ((), ()))


def each(count, body):
    def step(index, carry):
        body(index)
        return carry

    lax.fori_loop(0, count, step, 0)


def kernel(
    S, T, C, G, L, K, scales,
    grad_hbm, resid_hbm, weight_hbm, clean_hbm, corrupt_hbm, patched_hbm,
    scores,
    grad, resid, weight, clean, corrupt, patched,
    partner_grad, partner_resid, means, diff, unit, partial, partial_in, mask, acc, token, token_in,
    message, message_in, ending, ending_in, counts, scored, score_out,
    load_sem, piece_sem, weight_sem, pair_send, pair_recv, outer_send, inner_send, mean_recv, diff_send, diff_recv,
    part_send, part_recv, msg_send, msg_recv, end_send, end_recv, tok_send, tok_recv,
    turn, slice_send, slice_recv,
):
    assert T == 4
    seq = lax.axis_index("seq")
    tp = lax.axis_index("tp")
    pairs = S // 2
    partner = lax.rem(seq + pairs, S)
    upper = seq // pairs
    rows = grad.shape[0]
    half = rows // 2
    units = weight.shape[0]
    piece = units // C
    local_len = diff.shape[2]
    assert C <= K

    lanes = patched.shape[2]
    chunk = rows // K
    barrier = pltpu.get_barrier_semaphore()

    outer = pairs // 2
    mine = lax.rem(seq, pairs)
    chip = mine // 2
    core = lax.rem(mine, 2)

    sibling = upper * pairs + chip * 2 + 1 - core
    at_end = (tp == 0) | (tp == T - 1)
    single = local_len == rows
    first = core
    if single:
        first = jnp.where(tp == 0, 1, jnp.where(tp == T - 1, 0, core))
    leads = at_end & (core == first) & single
    follows = at_end & (core != first)

    def greet(i, j):
        pl.semaphore_signal(
            barrier, inc=1, device_id=(i, j), device_id_type=pl.DeviceIdType.MESH
        )

    def piece_rows(c):
        return pl.ds(pl.multiple_of(c * piece, 16), piece)

    def chunk_rows(k):
        return pl.ds(pl.multiple_of(k * chunk, 16), chunk)

    def local(source, target, index):
        return pltpu.make_async_copy(source, target, load_sem.at[index])

    grad_load = local(grad_hbm, grad, 0)
    resid_load = local(resid_hbm, resid, 1)

    def hidden_load(c):
        r = piece_rows(c)
        return (
            pltpu.make_async_copy(clean_hbm.at[r], clean.at[r], piece_sem.at[0, c]),
            pltpu.make_async_copy(corrupt_hbm.at[r], corrupt.at[r], piece_sem.at[1, c]),
        )

    def start_hidden(c):
        for load in hidden_load(c):
            load.start()

    def ids_load(k):
        return local(patched_hbm.at[pl.ds(pl.multiple_of(k * lanes, lanes), lanes)], patched.at[k, 0], 2 + k)

    def weight_load(c):
        return pltpu.make_async_copy(
            weight_hbm.at[piece_rows(c)], weight.at[piece_rows(c)], weight_sem.at[c]
        )

    start_hidden(0)
    each(T - 1, lambda i: greet(seq, lax.rem(tp + i + 1, T)))
    greet(partner, tp)
    greet(sibling, tp)
    each(outer - 1, lambda i: greet(upper * pairs + lax.rem(chip + i + 1, outer) * 2 + core, tp))
    grad_load.start()
    each(C - 1, lambda c: start_hidden(c + 1))
    each(patched.shape[0], lambda k: ids_load(k).start())

    def remote(source, target, send, recv, device):
        return pltpu.make_async_remote_copy(
            src_ref=source, dst_ref=target, send_sem=send, recv_sem=recv,
            device_id=device, device_id_type=pl.DeviceIdType.MESH,
        )

    keep = pl.ds(pl.multiple_of(upper * half, 8), half)
    give = pl.ds(pl.multiple_of((1 - upper) * half, 8), half)

    def grad_copy(k):
        r = chunk_rows(k)
        return remote(
            grad.at[r], partner_grad.at[r], pair_send.at[k], pair_recv.at[k], (partner, tp)
        )

    resid_copy = remote(
        resid.at[give], partner_resid, pair_send.at[K], pair_recv.at[K], (partner, tp)
    )
    score_copy = remote(
        score_out, scored.at[upper], pair_send.at[K + 1], pair_recv.at[K + 1], (partner, tp)
    )

    def diff_copy(block, c, step):
        place = diff.at[block, piece_rows(c)]
        direction = (step + 1) // 2
        return remote(
            place, place, diff_send.at[direction, block, c], diff_recv.at[block, c],
            (seq, tp + step),
        )

    def forward(block, c, step):
        @pl.when((tp + step >= 0) & (tp + step < T))
        def _():
            diff_copy(block, c, step).start()

    def own(c):
        @pl.when((tp != 1) | (c < C - 1))
        def _():
            forward(tp, c, 1)

        forward(tp, c, -1)

    def subtract(c):
        for load in hidden_load(c):
            load.wait()
        r = piece_rows(c)
        diff[tp, r, :] = (clean[r, :].astype(F32) - corrupt[r, :].astype(F32)).astype(BF16)
        own(c)

    pl.semaphore_wait(barrier, T + outer)
    subtract(0)
    grad_load.wait()

    @pl.when(~follows)
    def _():
        each(K, lambda k: grad_copy(k).start())

    each(C - 1, lambda c: subtract(c + 1))

    resid_load.start()
    each(C, lambda c: weight_load(c).start())

    def relay(c):
        @pl.when((tp >= 1) & ((tp != 2) | (c < C - 1)))
        def _():
            diff_copy(tp - 1, c, 1).wait_recv()

            @pl.when((tp == 2) & (c == C - 2))
            def _():
                diff_copy(0, 0, 1).wait_recv()
                forward(0, 0, 1)

            forward(tp - 1, c, 1)

        @pl.when(tp + 1 < T)
        def _():
            diff_copy(tp + 1, c, -1).wait_recv()

            @pl.when(tp >= 1)
            def _():
                forward(tp + 1, c, -1)

    def await_far(c):
        @pl.when(((tp == 2) & (c > 0)) | ((tp == 3) & (c < C - 2)))
        def _():
            diff_copy(tp - 2, c, 1).wait_recv()

        @pl.when(tp < 2)
        def _():
            diff_copy(tp + 2, c, -1).wait_recv()

    def mean_copy(block, h, send, target):
        place = means.at[lax.rem(block, 2) * outer + block // 2, chunk_rows(h)]
        return remote(place, place, send, mean_recv.at[block, h], (upper * pairs + target, tp))

    def outer_copy(i, h):
        return mean_copy(mine, h, outer_send.at[i, h], lax.rem(chip + i, outer) * 2 + core)

    def inner_copy(i, h):
        block = lax.rem(chip + i, outer) * 2 + core
        return mean_copy(block, h, inner_send.at[i, h], chip * 2 + 1 - core)

    def await_mean(block, h):
        mean_copy(block, h, inner_send.at[0, h], chip * 2 + 1 - core).wait_recv()

    counts[...] = jnp.zeros_like(counts)
    group_ids = lax.broadcasted_iota(jnp.int32, (G, lanes), 0)
    lane_ids = lax.broadcasted_iota(jnp.int32, (L, lanes), 0)

    def count(k):
        ids = patched[k] - seq * units + S * units
        high = ids // L - (S * units) // L
        low = lax.rem(ids, L)
        counts[...] += lax.dot_general(
            jnp.where(high == group_ids, 1.0, 0.0).astype(BF16),
            jnp.where(low == lane_ids, 1.0, 0.0).astype(BF16),
            NT, preferred_element_type=F32,
        )

    def spread(g):
        row = jnp.broadcast_to(counts[pl.ds(g, 1), :], (128, L))
        mask[pl.ds(pl.multiple_of(g * L, 8), L), :] = row.T

    def average(k):
        grad_copy(k).wait_recv()
        r = chunk_rows(k)
        both = grad[r, :].astype(F32) + partner_grad[r, :].astype(F32)
        means[core * outer + chip, r, :] = (both * 0.5).astype(BF16)
        each(outer - 1, lambda i: outer_copy(i + 1, k).start())
        inner_copy(0, k).start()

        @pl.when(leads & (k == 2))
        def _():
            pl.semaphore_signal(
                turn, inc=1, device_id=(sibling, tp), device_id_type=pl.DeviceIdType.MESH
            )

    def pass_on(k):
        def step(i):
            await_mean(lax.rem(chip + i + 1, outer) * 2 + core, k)
            inner_copy(i + 1, k).start()

        each(outer - 1, step)

    ids = patched.shape[0]
    ahead = max(ids - K, 0)
    each(ids, lambda k: ids_load(k).wait())
    each(ahead, count)

    @pl.when(follows)
    def _():
        pl.semaphore_wait(turn, 1)
        each(K, lambda k: grad_copy(k).start())

    def count_beside(k):
        @pl.when(ahead + k < ids)
        def _():
            count(ahead + k)

    for k in range(2):
        average(k)
        count_beside(k)

    def average_and_pass(k):
        average(k + 2)

        @pl.when(~follows)
        def _():
            pass_on(k)

        count_beside(k + 2)

    each(K - 2, average_and_pass)
    resid_load.wait()
    resid_copy.start()
    each(C // 2, relay)
    each(G, spread)
    acc[...] = jnp.zeros_like(acc)
    token[...] = jnp.zeros_like(token)

    def await_inner(k):
        each(outer, lambda i: await_mean(lax.rem(chip + i, outer) * 2 + 1 - core, k))

    @pl.when(~follows)
    def _():
        pass_on(K - 2)
        pass_on(K - 1)

    @pl.when(follows)
    def _():
        each(K, await_inner)

    far = jnp.where(tp == 0, T - 1, 0)
    inward = jnp.where(tp == 0, 1, -1)

    def partial_copy(c):
        r = piece_rows(c)
        return remote(
            partial.at[r], partial_in.at[r], part_send.at[c], part_recv.at[c], (seq, tp + inward)
        )

    def multiply(side, c):
        r = piece_rows(c)
        right = means[pl.ds(side * outer, outer)]
        right = right.reshape(outer * rows, right.shape[-1])
        result = lax.dot_general(weight[r, :], right, NT, preferred_element_type=F32)
        for j in range(outer):
            part = result[:, j * rows : (j + 1) * rows]
            if single:
                unit[2 * j + side, r, :] = part
            else:
                place = (2 * j + side) * rows
                columns = pl.ds(pl.multiple_of(lax.rem(place, local_len), 128), rows)
                unit[place // local_len, r, columns] = part

    def export(block, source, slot):
        partial[piece_rows(slot), :] = unit[block, piece_rows(source), :].astype(BF16)
        partial_copy(slot).start()

    def ship(c):
        @pl.when((tp == 0) | ((tp == T - 1) & (c > 0)))
        def _():
            export(far, c, c)

    def multiply_first(c):
        weight_load(c).wait()
        multiply(first, c)
        if single:
            ship(c)

        @pl.when(follows)
        def _():
            pass_on(c)

    each(C // 2, multiply_first)

    def multiply_and_relay(c):
        multiply_first(c + C // 2)
        relay(c + C // 2)

    each(C - C // 2, multiply_and_relay)

    per = G // C
    kept = G - per

    def slice_rows(g):
        return pl.ds((kept + g) * L, L)

    def slice_copy(g):
        place = diff.at[1, slice_rows(g)]
        return remote(place, place, slice_send.at[g], slice_recv.at[g], (seq, 2))

    @pl.when(tp == 1)
    def _():
        for g in range(per):
            slice_copy(g).start()

    @pl.when(follows)
    def _():
        each(K - C, lambda k: pass_on(k + C))

    @pl.when(~follows)
    def _():
        each(K, await_inner)

    def multiply_second(c):
        multiply(1 - first, c)
        if not single:
            ship(c)

        @pl.when((tp == T - 1) & (c == C - 1))
        def _():
            export(1, C - 1, 0)

    each(C, multiply_second)

    def product(block, c):
        product_rows(block, piece_rows(c))

    def product_rows(block, r):
        value = diff[block, r, :].astype(F32) * unit[block, r, :]
        masks = mask[r, :]
        for k in range(local_len // 128):
            part = value[:, k * 128 : (k + 1) * 128]
            acc[r, :] += part
            token[block, :, k * 128 : (k + 1) * 128] += jnp.sum(
                part * masks, axis=0, keepdims=True
            )

    def products(s, c):
        if s == 0:
            product(tp, c)
            return

        if s == 1:
            left = (tp >= 1) & ((tp != 2) | (c < C - 1))
        else:
            left = (tp == 2) | ((tp == 3) & (c < C - 2))

        @pl.when(left)
        def _():
            product(tp - s, c)

        @pl.when(tp + s < T)
        def _():
            product(tp + s, c)

    resid_copy.wait()
    sign = (1 - 2 * upper).astype(F32)

    difference = sign * (resid[keep, :].astype(F32) - partner_resid[...].astype(F32))

    def score(gradient):
        terms = difference * gradient.astype(F32)
        folded = terms[:, 0:128]
        for j in range(1, terms.shape[1] // 128):
            folded = folded + terms[:, j * 128 : (j + 1) * 128]
        return jnp.sum(folded.T, axis=0, keepdims=True)

    score_out[...] = score(partner_grad[keep, :])
    score_copy.start()
    scored[upper] = score(grad[keep, :])
    each(C, lambda c: products(0, c))
    each(C, lambda c: products(1, c))
    def await_help(slot):
        part = piece_rows(slot)
        remote(
            partial.at[part], partial_in.at[part], part_send.at[slot], part_recv.at[slot],
            (seq, jnp.where(tp == 1, 0, T - 1)),
        ).wait_recv()

    def help_in(c):
        @pl.when((tp == 1) | ((tp == 2) & (c > 0)))
        def _():
            await_help(c)
            r = piece_rows(c)
            unit[jnp.where(tp == 1, T - 1, 0), r, :] += partial_in[r, :].astype(F32)

    def fold(g, target, row):
        block = acc[pl.ds(pl.multiple_of(g * L, 8), L), :]
        target[pl.ds(row, 1), :] = jnp.sum(block.T, axis=0, keepdims=True)

    score_copy.wait()
    message[kept:, :] = jnp.zeros((2, L), F32)
    for k in range(2):
        message[kept + k : kept + k + 1, 0:half] = scored[k]

    me = seq * T + tp
    other = jnp.where(tp == 3, 2, tp + 1)
    middle = jnp.where(tp == 0, 3, 0)
    late = jnp.where(tp < 2, tp + 2, 1)

    def token_copy(s, block):
        return remote(
            token.at[block], token_in.at[me], tok_send.at[0], tok_recv.at[0], (s, block)
        )

    def send_tokens(block):
        each(S, lambda i: token_copy(lax.rem(seq + i, S), block).start())

    each(S - 1, lambda i: token_copy(lax.rem(seq + i + 1, S), tp).start())
    send_tokens(other)

    @pl.when(tp < 2)
    def _():
        send_tokens(middle)

    token_in[me] = token[tp]

    def last(c):
        await_far(c)
        help_in(c)
        products(2, c)

    def last_and_fold(c):
        last(c)
        each(per, lambda g: fold(c * per + g, message, c * per + g))

    def sent_means(k):
        grad_copy(k).wait_send()
        each(outer - 1, lambda i: outer_copy(i + 1, k).wait_send())
        each(outer, lambda i: inner_copy(i, k).wait_send())

    def drain_own(c):
        @pl.when((tp < T - 1) & ((tp != 1) | (c < C - 1)))
        def _():
            diff_copy(tp, c, 1).wait_send()

        @pl.when(tp > 0)
        def _():
            diff_copy(tp, c, -1).wait_send()

    def drain_relay(c):
        @pl.when((tp == 1) | ((tp == 2) & (c < C - 1)))
        def _():
            diff_copy(tp - 1, c, 1).wait_send()

        @pl.when((tp == 1) | (tp == 2))
        def _():
            diff_copy(tp + 1, c, -1).wait_send()

    each(K, sent_means)
    each(C, drain_own)
    each(C - 1, last_and_fold)

    def share(source, target, send, recv, i):
        return remote(source, target.at[tp], send.at[i], recv.at[tp], (seq, lax.rem(tp + i, T)))

    def message_copy(i):
        return share(message, message_in, msg_send, msg_recv, i)

    def ending_copy(i):
        return share(ending, ending_in, end_send, end_recv, i)

    def send_message():
        each(T - 1, lambda i: message_copy(i + 1).start())

    @pl.when(tp < 3)
    def _():
        send_message()

    def send_ending():
        each(T - 1, lambda i: ending_copy(i + 1).start())

    def end(group):
        for g in range(per):
            fold(group + g, ending, g)
        send_ending()

    last(C - 1)

    @pl.when(tp == 2)
    def _():
        send_tokens(0)
        await_help(0)
        unit[1, piece_rows(C - 1), :] += partial_in[piece_rows(0), :].astype(F32)
        for g in range(per):
            slice_copy(g).wait_recv()
            product_rows(1, slice_rows(g))
            fold(kept + g, ending, g)
        send_ending()

    @pl.when(tp == 3)
    def _():
        diff_copy(0, 0, 1).wait_recv()
        product(0, 0)
        send_tokens(0)
        for g in range(per):
            fold(g, message, g)
            fold(kept + g, message, kept - per + g)
        send_message()
        diff_copy(1, C - 2, 1).wait_recv()
        product(1, C - 2)
        end(kept - per)

    @pl.when(tp < 2)
    def _():
        end(kept)

    send_tokens(late)
    message_in[tp] = message[...]
    ending_in[tp] = ending[...]

    @pl.when(at_end)
    def _():
        each(C, lambda c: partial_copy(c).wait_send())

    each(C, drain_relay)

    @pl.when(tp == 1)
    def _():
        for g in range(per):
            slice_copy(g).wait_send()

    @pl.when(tp == 2)
    def _():
        diff_copy(0, 0, 1).wait_send()

    def await_message(i):
        source = lax.rem(tp + i + 1, T)
        remote(
            message, message_in.at[source], msg_send.at[0], msg_recv.at[source], (seq, source)
        ).wait_recv()

    each(T - 1, await_message)
    total = jnp.sum(message_in[...], axis=0)
    split = kept - per
    scores[0:split, :] = total[:split] * scales[2]
    scores[G : G + 2, :] = total[kept:] * scales[0]

    each(T - 1, lambda i: message_copy(i + 1).wait_send())

    def await_ending(i):
        source = lax.rem(tp + i + 1, T)
        remote(
            ending, ending_in.at[source], end_send.at[0], end_recv.at[source], (seq, source)
        ).wait_recv()

    each(T - 1, await_ending)
    rest = jnp.sum(message_in[0:3, split:kept, :], axis=0) + ending_in[3]
    scores[split:kept, :] = rest * scales[2]
    rest = jnp.sum(ending_in[0:3], axis=0) + message_in[3, split:kept, :]
    scores[kept:G, :] = rest * scales[2]
    others = token_in.at[pl.ds(0, S * T - 1)]
    tokens = remote(others, others, tok_send.at[0], tok_recv.at[0], (seq, tp))
    tokens.wait_recv()
    token_total = jnp.sum(token_in[...], axis=0) * scales[1]
    for k in range(local_len // L):
        scores[G + 2 + k : G + 3 + k, :] = token_total[:, k * L : (k + 1) * L]

    tokens.wait_send()
    each(T - 1, lambda i: ending_copy(i + 1).wait_send())


def write(G, K, L, half, scores, resid_out, token_out, neuron_out):
    for k in range(2):
        resid_out[k * half : (k + 1) * half] = scores[G + k, 0:half]
    for k in range(K):
        token_out[k * L : (k + 1) * L] = scores[G + 2 + k, :]
    for g in range(G):
        neuron_out[g * L : (g + 1) * L] = scores[g, :]


def shards(grad_out, resid_in, down_weight, hidden_clean, hidden_corrupt, patched):
    S = lax.axis_size("seq")
    T = lax.axis_size("tp")
    rows, width = grad_out.shape
    units, local_len = hidden_clean.shape
    L = math.gcd(units, 128)
    G = units // L
    C = max(c for c in range(1, 9) if G % c == 0)
    lanes = math.gcd(patched.shape[0], 1024)
    half = rows // 2
    scales = (
        1.0 / math.sqrt(width * T),
        1.0 / math.sqrt(patched.shape[0]),
        1.0 / math.sqrt(local_len * T),
    )
    dma = lambda *shape: pltpu.SemaphoreType.DMA(shape)
    K = local_len // L
    chunks = rows // 16
    scores = pl.pallas_call(
        functools.partial(kernel, S, T, C, G, L, chunks, scales),
        out_shape=pltpu.VMEM((G + 2 + K, L), F32),
        in_specs=[pl.BlockSpec(memory_space=pl.ANY)] * 6,
        out_specs=pl.BlockSpec(memory_space=pltpu.VMEM),
        scratch_shapes=[
            pltpu.VMEM((rows, width), BF16),
            pltpu.VMEM((rows, width), BF16),
            pltpu.VMEM((units, width), BF16),
            pltpu.VMEM((units, local_len), BF16),
            pltpu.VMEM((units, local_len), BF16),
            pltpu.VMEM((patched.shape[0] // lanes, 1, lanes), jnp.int32),
            pltpu.VMEM((rows, width), BF16),
            pltpu.VMEM((half, width), BF16),
            pltpu.VMEM((S // 2, rows, width), BF16),
            pltpu.VMEM((T, units, local_len), BF16),
            pltpu.VMEM((T, units, local_len), F32),
            pltpu.VMEM((units, local_len), BF16),
            pltpu.VMEM((units, local_len), BF16),
            pltpu.VMEM((units, 128), F32),
            pltpu.VMEM((units, 128), F32),
            pltpu.VMEM((T, 1, local_len), F32),
            pltpu.VMEM((S * T, 1, local_len), F32),
            pltpu.VMEM((G - G // C + 2, L), F32),
            pltpu.VMEM((T, G - G // C + 2, L), F32),
            pltpu.VMEM((G // C, L), F32),
            pltpu.VMEM((T, G // C, L), F32),
            pltpu.VMEM((G, L), F32),
            pltpu.VMEM((2, 1, half), F32),
            pltpu.VMEM((1, half), F32),
            dma(2 + patched.shape[0] // lanes), dma(2, C), dma(C), dma(chunks + 2), dma(chunks + 2),
            dma(S // 4, chunks), dma(S // 4, chunks), dma(S // 2, chunks),
            dma(2, T, C), dma(T, C), dma(C), dma(C),
            dma(T), dma(T), dma(T), dma(T), dma(1), dma(1),
            pltpu.SemaphoreType.REGULAR, dma(G // C), dma(G // C),
        ],
        compiler_params=pltpu.CompilerParams(
            collective_id=0, has_side_effects=True, vmem_limit_bytes=56 * 1024 * 1024
        ),
    )(
        grad_out, resid_in, down_weight, hidden_clean, hidden_corrupt,
        patched,
    )
    return pl.pallas_call(
        functools.partial(write, G, K, L, half),
        out_shape=(
            jax.ShapeDtypeStruct((rows,), F32),
            jax.ShapeDtypeStruct((local_len,), F32),
            jax.ShapeDtypeStruct((units,), F32),
        ),
        in_specs=[pl.BlockSpec(memory_space=pltpu.VMEM)],
        out_specs=[pl.BlockSpec(memory_space=pltpu.VMEM)] * 3,
    )(pltpu.with_memory_space_constraint(scores, pltpu.VMEM))


def solution(mesh):
    in_specs = (P("seq", "tp"), P("seq", "tp"), P("seq", "tp"), P("seq", "tp"), P("seq", "tp"), P())
    out_specs = (P("seq"), P("tp"), P("seq"))
    return jax.shard_map(shards, mesh=mesh, in_specs=in_specs, out_specs=out_specs, check_vma=False)
```

```python
import functools
import math

import jax
import jax.numpy as jnp
from jax import lax
from jax.experimental import pallas as pl
from jax.experimental.pallas import tpu as pltpu
from jax.sharding import PartitionSpec as P

F32 = jnp.float32
BF16 = jnp.bfloat16
NT = (((1,), (1,)), ((), ()))


def each(count, body):
    def step(index, carry):
        body(index)
        return carry

    lax.fori_loop(0, count, step, 0)


def few(count, body):
    if count > 8:
        each(count, body)
        return
    for index in range(count):
        body(index)


def kernel(
    S, T, C, G, L, K, scales,
    grad_hbm, resid_hbm, weight_hbm, clean_hbm, corrupt_hbm, patched_hbm,
    scores,
    grad, resid, weight, clean, corrupt, patched,
    partner_grad, partner_resid, means, diff, unit, partial, partial_in, mask, acc, token, token_in,
    message, message_in, ending, ending_in, counts, scored, score_out,
    load_sem, piece_sem, weight_sem, pair_send, pair_recv, outer_send, inner_send, mean_recv, diff_send, diff_recv,
    part_send, part_recv, msg_send, msg_recv, end_send, end_recv, tok_send, tok_recv,
    turn, slice_send, slice_recv,
):
    assert T == 4
    seq = lax.axis_index("seq")
    tp = lax.axis_index("tp")
    pairs = S // 2
    partner = lax.rem(seq + pairs, S)
    upper = seq // pairs
    rows = grad.shape[0]
    half = rows // 2
    units = weight.shape[0]
    piece = units // C
    local_len = diff.shape[2]
    assert C <= K

    lanes = patched.shape[2]
    chunk = rows // K
    barrier = pltpu.get_barrier_semaphore()

    outer = pairs // 2
    mine = lax.rem(seq, pairs)
    chip = mine // 2
    core = lax.rem(mine, 2)

    sibling = upper * pairs + chip * 2 + 1 - core
    at_end = (tp == 0) | (tp == T - 1)
    single = local_len == rows
    first = core
    if single:
        first = jnp.where(tp == 0, 1, jnp.where(tp == T - 1, 0, core))
    leads = at_end & (core == first) & single
    follows = at_end & (core != first)

    def greet(i, j):
        pl.semaphore_signal(
            barrier, inc=1, device_id=(i, j), device_id_type=pl.DeviceIdType.MESH
        )

    def piece_rows(c):
        return pl.ds(pl.multiple_of(c * piece, 16), piece)

    def chunk_rows(k):
        return pl.ds(pl.multiple_of(k * chunk, 16), chunk)

    def local(source, target, index):
        return pltpu.make_async_copy(source, target, load_sem.at[index])

    grad_load = local(grad_hbm, grad, 0)
    resid_load = local(resid_hbm, resid, 1)

    def hidden_load(c):
        r = piece_rows(c)
        return (
            pltpu.make_async_copy(clean_hbm.at[r], clean.at[r], piece_sem.at[0, c]),
            pltpu.make_async_copy(corrupt_hbm.at[r], corrupt.at[r], piece_sem.at[1, c]),
        )

    def start_hidden(c):
        for load in hidden_load(c):
            load.start()

    def ids_load(k):
        return local(patched_hbm.at[pl.ds(pl.multiple_of(k * lanes, lanes), lanes)], patched.at[k, 0], 2 + k)

    def weight_load(c):
        return pltpu.make_async_copy(
            weight_hbm.at[piece_rows(c)], weight.at[piece_rows(c)], weight_sem.at[c]
        )

    few(T - 1, lambda i: greet(seq, lax.rem(tp + T - 1 - i, T)))
    greet(partner, tp)
    greet(sibling, tp)
    few(outer - 1, lambda i: greet(upper * pairs + lax.rem(chip + i + 1, outer) * 2 + core, tp))
    start_hidden(0)
    grad_load.start()
    each(C - 1, lambda c: start_hidden(c + 1))
    each(patched.shape[0], lambda k: ids_load(k).start())

    def remote(source, target, send, recv, device):
        return pltpu.make_async_remote_copy(
            src_ref=source, dst_ref=target, send_sem=send, recv_sem=recv,
            device_id=device, device_id_type=pl.DeviceIdType.MESH,
        )

    keep = pl.ds(pl.multiple_of(upper * half, 8), half)
    give = pl.ds(pl.multiple_of((1 - upper) * half, 8), half)

    def grad_copy(k):
        r = chunk_rows(k)
        return remote(
            grad.at[r], partner_grad.at[r], pair_send.at[k], pair_recv.at[k], (partner, tp)
        )

    resid_copy = remote(
        resid.at[give], partner_resid, pair_send.at[K], pair_recv.at[K], (partner, tp)
    )
    score_copy = remote(
        score_out, scored.at[upper], pair_send.at[K + 1], pair_recv.at[K + 1], (partner, tp)
    )

    def diff_copy(block, c, step):
        place = diff.at[block, piece_rows(c)]
        direction = (step + 1) // 2
        return remote(
            place, place, diff_send.at[direction, block, c], diff_recv.at[block, c],
            (seq, tp + step),
        )

    def forward(block, c, step):
        @pl.when((tp + step >= 0) & (tp + step < T))
        def _():
            diff_copy(block, c, step).start()

    def own(c):
        @pl.when((tp != 1) | (c < C - 1))
        def _():
            forward(tp, c, 1)

        forward(tp, c, -1)

    def subtract(c):
        for load in hidden_load(c):
            load.wait()
        r = piece_rows(c)
        diff[tp, r, :] = (clean[r, :].astype(F32) - corrupt[r, :].astype(F32)).astype(BF16)
        own(c)

    pl.semaphore_wait(barrier, T + outer)
    subtract(0)
    grad_load.wait()

    @pl.when(~follows)
    def _():
        each(K, lambda k: grad_copy(k).start())

    each(C - 1, lambda c: subtract(c + 1))

    resid_load.start()
    each(C, lambda c: weight_load(c).start())

    def relay(c):
        @pl.when((tp >= 1) & ((tp != 2) | (c < C - 1)))
        def _():
            diff_copy(tp - 1, c, 1).wait_recv()

            @pl.when((tp == 2) & (c == C - 2))
            def _():
                diff_copy(0, 0, 1).wait_recv()
                forward(0, 0, 1)

            forward(tp - 1, c, 1)

        @pl.when(tp + 1 < T)
        def _():
            diff_copy(tp + 1, c, -1).wait_recv()

            @pl.when(tp >= 1)
            def _():
                forward(tp + 1, c, -1)

    def await_far(c):
        @pl.when(((tp == 2) & (c > 0)) | ((tp == 3) & (c < C - 2)))
        def _():
            diff_copy(tp - 2, c, 1).wait_recv()

        @pl.when(tp < 2)
        def _():
            diff_copy(tp + 2, c, -1).wait_recv()

    def mean_copy(block, h, send, target):
        place = means.at[lax.rem(block, 2) * outer + block // 2, chunk_rows(h)]
        return remote(place, place, send, mean_recv.at[block, h], (upper * pairs + target, tp))

    def outer_copy(i, h):
        return mean_copy(mine, h, outer_send.at[i, h], lax.rem(chip + i, outer) * 2 + core)

    def inner_copy(i, h):
        block = lax.rem(chip + i, outer) * 2 + core
        return mean_copy(block, h, inner_send.at[i, h], chip * 2 + 1 - core)

    def await_mean(block, h):
        mean_copy(block, h, inner_send.at[0, h], chip * 2 + 1 - core).wait_recv()

    counts[...] = jnp.zeros_like(counts)
    group_ids = lax.broadcasted_iota(jnp.int32, (G, lanes), 0)
    lane_ids = lax.broadcasted_iota(jnp.int32, (L, lanes), 0)

    def count(k):
        ids = patched[k] - seq * units + S * units
        high = ids // L - (S * units) // L
        low = lax.rem(ids, L)
        counts[...] += lax.dot_general(
            jnp.where(high == group_ids, 1.0, 0.0).astype(BF16),
            jnp.where(low == lane_ids, 1.0, 0.0).astype(BF16),
            NT, preferred_element_type=F32,
        )

    def spread(g):
        row = jnp.broadcast_to(counts[pl.ds(g, 1), :], (128, L))
        mask[pl.ds(pl.multiple_of(g * L, 8), L), :] = row.T

    def average(k):
        grad_copy(k).wait_recv()
        r = chunk_rows(k)
        both = grad[r, :].astype(F32) + partner_grad[r, :].astype(F32)
        means[core * outer + chip, r, :] = (both * 0.5).astype(BF16)
        few(outer - 1, lambda i: outer_copy(i + 1, k).start())
        inner_copy(0, k).start()

        @pl.when(leads & (k == 2))
        def _():
            pl.semaphore_signal(
                turn, inc=1, device_id=(sibling, tp), device_id_type=pl.DeviceIdType.MESH
            )

    def pass_on(k):
        def step(i):
            await_mean(lax.rem(chip + i + 1, outer) * 2 + core, k)
            inner_copy(i + 1, k).start()

        few(outer - 1, step)

    ids = patched.shape[0]
    ahead = max(ids - K, 0)
    each(ids, lambda k: ids_load(k).wait())
    each(ahead, count)

    @pl.when(follows)
    def _():
        pl.semaphore_wait(turn, 1)
        each(K, lambda k: grad_copy(k).start())

    def count_beside(k):
        @pl.when(ahead + k < ids)
        def _():
            count(ahead + k)

    for k in range(2):
        average(k)
        count_beside(k)

    def average_and_pass(k):
        average(k + 2)

        @pl.when(~follows)
        def _():
            pass_on(k)

        count_beside(k + 2)

    each(K - 2, average_and_pass)
    resid_load.wait()
    resid_copy.start()
    each(C // 2, relay)
    each(G, spread)
    acc[...] = jnp.zeros_like(acc)
    token[...] = jnp.zeros_like(token)

    def await_inner(k):
        few(outer, lambda i: await_mean(lax.rem(chip + i, outer) * 2 + 1 - core, k))

    @pl.when(~follows)
    def _():
        pass_on(K - 2)
        pass_on(K - 1)

    @pl.when(follows)
    def _():
        each(K, await_inner)

    far = jnp.where(tp == 0, T - 1, 0)
    inward = jnp.where(tp == 0, 1, -1)

    def partial_copy(c):
        r = piece_rows(c)
        return remote(
            partial.at[r], partial_in.at[r], part_send.at[c], part_recv.at[c], (seq, tp + inward)
        )

    def multiply(side, c):
        r = piece_rows(c)
        right = means[pl.ds(side * outer, outer)]
        right = right.reshape(outer * rows, right.shape[-1])
        result = lax.dot_general(weight[r, :], right, NT, preferred_element_type=F32)
        for j in range(outer):
            part = result[:, j * rows : (j + 1) * rows]
            if single:
                unit[2 * j + side, r, :] = part
            else:
                place = (2 * j + side) * rows
                columns = pl.ds(pl.multiple_of(lax.rem(place, local_len), 128), rows)
                unit[place // local_len, r, columns] = part

    def export(block, source, slot):
        partial[piece_rows(slot), :] = unit[block, piece_rows(source), :].astype(BF16)
        partial_copy(slot).start()

    def ship(c):
        @pl.when((tp == 0) | ((tp == T - 1) & (c > 0)))
        def _():
            export(far, c, c)

    def multiply_first(c):
        weight_load(c).wait()
        multiply(first, c)
        if single:
            ship(c)

        @pl.when(follows)
        def _():
            pass_on(c)

    each(C // 2, multiply_first)

    def multiply_and_relay(c):
        multiply_first(c + C // 2)
        relay(c + C // 2)

    each(C - C // 2, multiply_and_relay)

    per = G // C
    kept = G - per

    def slice_rows(g):
        return pl.ds((kept + g) * L, L)

    def slice_copy(g):
        place = diff.at[1, slice_rows(g)]
        return remote(place, place, slice_send.at[g], slice_recv.at[g], (seq, 2))

    @pl.when(tp == 1)
    def _():
        for g in range(per):
            slice_copy(g).start()

    @pl.when(follows)
    def _():
        each(K - C, lambda k: pass_on(k + C))

    @pl.when(~follows)
    def _():
        each(K, await_inner)

    def multiply_second(c):
        multiply(1 - first, c)
        if not single:
            ship(c)

        @pl.when((tp == T - 1) & (c == C - 1))
        def _():
            export(1, C - 1, 0)

    each(C, multiply_second)

    def product(block, c):
        product_rows(block, piece_rows(c))

    def product_rows(block, r):
        value = diff[block, r, :].astype(F32) * unit[block, r, :]
        masks = mask[r, :]
        for k in range(local_len // 128):
            part = value[:, k * 128 : (k + 1) * 128]
            acc[r, :] += part
            token[block, :, k * 128 : (k + 1) * 128] += jnp.sum(
                part * masks, axis=0, keepdims=True
            )

    def products(s, c):
        if s == 0:
            product(tp, c)
            return

        if s == 1:
            left = (tp >= 1) & ((tp != 2) | (c < C - 1))
        else:
            left = (tp == 2) | ((tp == 3) & (c < C - 2))

        @pl.when(left)
        def _():
            product(tp - s, c)

        @pl.when(tp + s < T)
        def _():
            product(tp + s, c)

    resid_copy.wait()
    sign = (1 - 2 * upper).astype(F32)

    difference = sign * (resid[keep, :].astype(F32) - partner_resid[...].astype(F32))

    def score(gradient):
        terms = difference * gradient.astype(F32)
        folded = terms[:, 0:128]
        for j in range(1, terms.shape[1] // 128):
            folded = folded + terms[:, j * 128 : (j + 1) * 128]
        return jnp.sum(folded.T, axis=0, keepdims=True)

    score_out[...] = score(partner_grad[keep, :])
    score_copy.start()
    scored[upper] = score(grad[keep, :])
    each(C, lambda c: products(0, c))
    each(C, lambda c: products(1, c))
    def await_help(slot):
        part = piece_rows(slot)
        remote(
            partial.at[part], partial_in.at[part], part_send.at[slot], part_recv.at[slot],
            (seq, jnp.where(tp == 1, 0, T - 1)),
        ).wait_recv()

    def help_in(c):
        @pl.when((tp == 1) | ((tp == 2) & (c > 0)))
        def _():
            await_help(c)
            r = piece_rows(c)
            unit[jnp.where(tp == 1, T - 1, 0), r, :] += partial_in[r, :].astype(F32)

    def fold(g, target, row):
        block = acc[pl.ds(pl.multiple_of(g * L, 8), L), :]
        target[pl.ds(row, 1), :] = jnp.sum(block.T, axis=0, keepdims=True)

    score_copy.wait()
    message[kept:, :] = jnp.zeros((2, L), F32)
    for k in range(2):
        message[kept + k : kept + k + 1, 0:half] = scored[k]

    me = seq * T + tp
    other = jnp.where(tp == 3, 2, tp + 1)
    middle = jnp.where(tp == 0, 3, 0)
    late = jnp.where(tp < 2, tp + 2, 1)

    def token_copy(s, block):
        return remote(
            token.at[block], token_in.at[me], tok_send.at[0], tok_recv.at[0], (s, block)
        )

    def send_tokens(block):
        few(S, lambda i: token_copy(lax.rem(seq + i, S), block).start())

    few(S - 1, lambda i: token_copy(lax.rem(seq + i + 1, S), tp).start())
    send_tokens(other)

    @pl.when(tp < 2)
    def _():
        send_tokens(middle)

    token_in[me] = token[tp]

    def last(c):
        await_far(c)
        help_in(c)
        products(2, c)

    def last_and_fold(c):
        last(c)
        each(per, lambda g: fold(c * per + g, message, c * per + g))

    def sent_means(k):
        grad_copy(k).wait_send()
        few(outer - 1, lambda i: outer_copy(i + 1, k).wait_send())
        few(outer, lambda i: inner_copy(i, k).wait_send())

    def drain_own(c):
        @pl.when((tp < T - 1) & ((tp != 1) | (c < C - 1)))
        def _():
            diff_copy(tp, c, 1).wait_send()

        @pl.when(tp > 0)
        def _():
            diff_copy(tp, c, -1).wait_send()

    def drain_relay(c):
        @pl.when((tp == 1) | ((tp == 2) & (c < C - 1)))
        def _():
            diff_copy(tp - 1, c, 1).wait_send()

        @pl.when((tp == 1) | (tp == 2))
        def _():
            diff_copy(tp + 1, c, -1).wait_send()

    each(K, sent_means)
    each(C, drain_own)
    each(C - 1, last_and_fold)

    def share(source, target, send, recv, i):
        return remote(source, target.at[tp], send.at[i], recv.at[tp], (seq, lax.rem(tp + i, T)))

    def message_copy(i):
        return share(message, message_in, msg_send, msg_recv, i)

    def ending_copy(i):
        return share(ending, ending_in, end_send, end_recv, i)

    def send_message():
        few(T - 1, lambda i: message_copy(i + 1).start())

    @pl.when(tp < 3)
    def _():
        send_message()

    def send_ending():
        few(T - 1, lambda i: ending_copy(i + 1).start())

    def end(group):
        for g in range(per):
            fold(group + g, ending, g)
        send_ending()

    last(C - 1)

    @pl.when(tp == 2)
    def _():
        send_tokens(0)
        await_help(0)
        unit[1, piece_rows(C - 1), :] += partial_in[piece_rows(0), :].astype(F32)
        for g in range(per):
            slice_copy(g).wait_recv()
            product_rows(1, slice_rows(g))
            fold(kept + g, ending, g)
        send_ending()

    @pl.when(tp == 3)
    def _():
        diff_copy(0, 0, 1).wait_recv()
        product(0, 0)
        send_tokens(0)
        for g in range(per):
            fold(g, message, g)
            fold(kept + g, message, kept - per + g)
        send_message()
        diff_copy(1, C - 2, 1).wait_recv()
        product(1, C - 2)
        end(kept - per)

    @pl.when(tp < 2)
    def _():
        end(kept)

    send_tokens(late)
    message_in[tp] = message[...]
    ending_in[tp] = ending[...]

    @pl.when(at_end)
    def _():
        each(C, lambda c: partial_copy(c).wait_send())

    each(C, drain_relay)

    @pl.when(tp == 1)
    def _():
        for g in range(per):
            slice_copy(g).wait_send()

    @pl.when(tp == 2)
    def _():
        diff_copy(0, 0, 1).wait_send()

    def await_message(i):
        source = lax.rem(tp + i + 1, T)
        remote(
            message, message_in.at[source], msg_send.at[0], msg_recv.at[source], (seq, source)
        ).wait_recv()

    few(T - 1, await_message)
    total = jnp.sum(message_in[...], axis=0)
    split = kept - per
    scores[0:split, :] = total[:split] * scales[2]
    scores[G : G + 2, :] = total[kept:] * scales[0]

    few(T - 1, lambda i: message_copy(i + 1).wait_send())

    def await_ending(i):
        source = lax.rem(tp + i + 1, T)
        remote(
            ending, ending_in.at[source], end_send.at[0], end_recv.at[source], (seq, source)
        ).wait_recv()

    few(T - 1, await_ending)
    rest = jnp.sum(message_in[0:3, split:kept, :], axis=0) + ending_in[3]
    scores[split:kept, :] = rest * scales[2]
    rest = jnp.sum(ending_in[0:3], axis=0) + message_in[3, split:kept, :]
    scores[kept:G, :] = rest * scales[2]
    others = token_in.at[pl.ds(0, S * T - 1)]
    tokens = remote(others, others, tok_send.at[0], tok_recv.at[0], (seq, tp))
    tokens.wait_recv()
    token_total = jnp.sum(token_in[...], axis=0) * scales[1]
    for k in range(local_len // L):
        scores[G + 2 + k : G + 3 + k, :] = token_total[:, k * L : (k + 1) * L]

    tokens.wait_send()
    few(T - 1, lambda i: ending_copy(i + 1).wait_send())


def write(G, K, L, half, scores, resid_out, token_out, neuron_out):
    for k in range(2):
        resid_out[k * half : (k + 1) * half] = scores[G + k, 0:half]
    for k in range(K):
        token_out[k * L : (k + 1) * L] = scores[G + 2 + k, :]
    for g in range(G):
        neuron_out[g * L : (g + 1) * L] = scores[g, :]


def shards(grad_out, resid_in, down_weight, hidden_clean, hidden_corrupt, patched):
    S = lax.axis_size("seq")
    T = lax.axis_size("tp")
    rows, width = grad_out.shape
    units, local_len = hidden_clean.shape
    L = math.gcd(units, 128)
    G = units // L
    C = max(c for c in range(1, 9) if G % c == 0)
    lanes = math.gcd(patched.shape[0], 1024)
    half = rows // 2
    scales = (
        1.0 / math.sqrt(width * T),
        1.0 / math.sqrt(patched.shape[0]),
        1.0 / math.sqrt(local_len * T),
    )
    dma = lambda *shape: pltpu.SemaphoreType.DMA(shape)
    K = local_len // L
    chunks = rows // 16
    scores = pl.pallas_call(
        functools.partial(kernel, S, T, C, G, L, chunks, scales),
        out_shape=pltpu.VMEM((G + 2 + K, L), F32),
        in_specs=[pl.BlockSpec(memory_space=pl.ANY)] * 6,
        out_specs=pl.BlockSpec(memory_space=pltpu.VMEM),
        scratch_shapes=[
            pltpu.VMEM((rows, width), BF16),
            pltpu.VMEM((rows, width), BF16),
            pltpu.VMEM((units, width), BF16),
            pltpu.VMEM((units, local_len), BF16),
            pltpu.VMEM((units, local_len), BF16),
            pltpu.VMEM((patched.shape[0] // lanes, 1, lanes), jnp.int32),
            pltpu.VMEM((rows, width), BF16),
            pltpu.VMEM((half, width), BF16),
            pltpu.VMEM((S // 2, rows, width), BF16),
            pltpu.VMEM((T, units, local_len), BF16),
            pltpu.VMEM((T, units, local_len), F32),
            pltpu.VMEM((units, local_len), BF16),
            pltpu.VMEM((units, local_len), BF16),
            pltpu.VMEM((units, 128), F32),
            pltpu.VMEM((units, 128), F32),
            pltpu.VMEM((T, 1, local_len), F32),
            pltpu.VMEM((S * T, 1, local_len), F32),
            pltpu.VMEM((G - G // C + 2, L), F32),
            pltpu.VMEM((T, G - G // C + 2, L), F32),
            pltpu.VMEM((G // C, L), F32),
            pltpu.VMEM((T, G // C, L), F32),
            pltpu.VMEM((G, L), F32),
            pltpu.VMEM((2, 1, half), F32),
            pltpu.VMEM((1, half), F32),
            dma(2 + patched.shape[0] // lanes), dma(2, C), dma(C), dma(chunks + 2), dma(chunks + 2),
            dma(S // 4, chunks), dma(S // 4, chunks), dma(S // 2, chunks),
            dma(2, T, C), dma(T, C), dma(C), dma(C),
            dma(T), dma(T), dma(T), dma(T), dma(1), dma(1),
            pltpu.SemaphoreType.REGULAR, dma(G // C), dma(G // C),
        ],
        compiler_params=pltpu.CompilerParams(
            collective_id=0, has_side_effects=True, vmem_limit_bytes=56 * 1024 * 1024
        ),
    )(
        grad_out, resid_in, down_weight, hidden_clean, hidden_corrupt,
        patched,
    )
    return pl.pallas_call(
        functools.partial(write, G, K, L, half),
        out_shape=(
            jax.ShapeDtypeStruct((rows,), F32),
            jax.ShapeDtypeStruct((local_len,), F32),
            jax.ShapeDtypeStruct((units,), F32),
        ),
        in_specs=[pl.BlockSpec(memory_space=pltpu.VMEM)],
        out_specs=[pl.BlockSpec(memory_space=pltpu.VMEM)] * 3,
    )(pltpu.with_memory_space_constraint(scores, pltpu.VMEM))


def solution(mesh):
    in_specs = (P("seq", "tp"), P("seq", "tp"), P("seq", "tp"), P("seq", "tp"), P("seq", "tp"), P())
    out_specs = (P("seq"), P("tp"), P("seq"))
    return jax.shard_map(shards, mesh=mesh, in_specs=in_specs, out_specs=out_specs, check_vma=False)
```

```python
import functools
import math

import jax
import jax.numpy as jnp
from jax import lax
from jax.experimental import pallas as pl
from jax.experimental.pallas import tpu as pltpu
from jax.sharding import PartitionSpec as P

F32 = jnp.float32
BF16 = jnp.bfloat16
NT = (((1,), (1,)), ((), ()))


def each(count, body):
    def step(index, carry):
        body(index)
        return carry

    lax.fori_loop(0, count, step, 0)


def kernel(
    S, T, C, G, L, K, scales,
    grad_hbm, resid_hbm, weight_hbm, clean_hbm, corrupt_hbm, patched_hbm,
    scores,
    grad, resid, weight, clean, corrupt, patched,
    partner_grad, partner_resid, means, diff, unit, partial, partial_in, mask, acc, token, token_in,
    message, message_in, ending, ending_in, counts, scored, score_out,
    load_sem, piece_sem, weight_sem, pair_send, pair_recv, outer_send, inner_send, mean_recv, diff_send, diff_recv,
    part_send, part_recv, msg_send, msg_recv, end_send, end_recv, tok_send, tok_recv,
    turn, slice_send, slice_recv,
):
    assert T == 4
    seq = lax.axis_index("seq")
    tp = lax.axis_index("tp")
    pairs = S // 2
    partner = lax.rem(seq + pairs, S)
    upper = seq // pairs
    rows = grad.shape[0]
    half = rows // 2
    units = weight.shape[0]
    piece = units // C
    local_len = diff.shape[2]
    assert C <= K

    lanes = patched.shape[2]
    chunk = rows // K
    barrier = pltpu.get_barrier_semaphore()

    outer = pairs // 2
    mine = lax.rem(seq, pairs)
    chip = mine // 2
    core = lax.rem(mine, 2)

    sibling = upper * pairs + chip * 2 + 1 - core
    at_end = (tp == 0) | (tp == T - 1)
    single = local_len == rows
    first = core
    if single:
        first = jnp.where(tp == 0, 1, jnp.where(tp == T - 1, 0, core))
    leads = at_end & (core == first) & single
    follows = at_end & (core != first)

    def greet(i, j):
        pl.semaphore_signal(
            barrier, inc=1, device_id=(i, j), device_id_type=pl.DeviceIdType.MESH
        )

    def piece_rows(c):
        return pl.ds(pl.multiple_of(c * piece, 16), piece)

    def chunk_rows(k):
        return pl.ds(pl.multiple_of(k * chunk, 16), chunk)

    def local(source, target, index):
        return pltpu.make_async_copy(source, target, load_sem.at[index])

    grad_load = local(grad_hbm, grad, 0)
    resid_load = local(resid_hbm, resid, 1)

    def hidden_load(c):
        r = piece_rows(c)
        return (
            pltpu.make_async_copy(clean_hbm.at[r], clean.at[r], piece_sem.at[0, c]),
            pltpu.make_async_copy(corrupt_hbm.at[r], corrupt.at[r], piece_sem.at[1, c]),
        )

    def start_hidden(c):
        for load in hidden_load(c):
            load.start()

    def ids_load(k):
        return local(patched_hbm.at[pl.ds(pl.multiple_of(k * lanes, lanes), lanes)], patched.at[k, 0], 2 + k)

    def weight_load(c):
        return pltpu.make_async_copy(
            weight_hbm.at[piece_rows(c)], weight.at[piece_rows(c)], weight_sem.at[c]
        )

    start_hidden(0)
    each(T - 1, lambda i: greet(seq, lax.rem(tp + i + 1, T)))
    greet(partner, tp)
    greet(sibling, tp)
    each(outer - 1, lambda i: greet(upper * pairs + lax.rem(chip + i + 1, outer) * 2 + core, tp))
    grad_load.start()
    each(C - 1, lambda c: start_hidden(c + 1))
    each(patched.shape[0], lambda k: ids_load(k).start())

    def remote(source, target, send, recv, device):
        return pltpu.make_async_remote_copy(
            src_ref=source, dst_ref=target, send_sem=send, recv_sem=recv,
            device_id=device, device_id_type=pl.DeviceIdType.MESH,
        )

    keep = pl.ds(pl.multiple_of(upper * half, 8), half)
    give = pl.ds(pl.multiple_of((1 - upper) * half, 8), half)

    def grad_copy(k):
        r = chunk_rows(k)
        return remote(
            grad.at[r], partner_grad.at[r], pair_send.at[k], pair_recv.at[k], (partner, tp)
        )

    resid_copy = remote(
        resid.at[give], partner_resid, pair_send.at[K], pair_recv.at[K], (partner, tp)
    )
    score_copy = remote(
        score_out, scored.at[upper], pair_send.at[K + 1], pair_recv.at[K + 1], (partner, tp)
    )

    def diff_copy(block, c, step):
        place = diff.at[block, piece_rows(c)]
        direction = (step + 1) // 2
        return remote(
            place, place, diff_send.at[direction, block, c], diff_recv.at[block, c],
            (seq, tp + step),
        )

    def forward(block, c, step):
        @pl.when((tp + step >= 0) & (tp + step < T))
        def _():
            diff_copy(block, c, step).start()

    def own(c):
        @pl.when((tp != 1) | (c < C - 1))
        def _():
            forward(tp, c, 1)

        forward(tp, c, -1)

    def subtract(c):
        for load in hidden_load(c):
            load.wait()
        r = piece_rows(c)
        diff[tp, r, :] = (clean[r, :].astype(F32) - corrupt[r, :].astype(F32)).astype(BF16)
        own(c)

    pl.semaphore_wait(barrier, T + outer)
    subtract(0)
    grad_load.wait()

    @pl.when(~follows)
    def _():
        each(K, lambda k: grad_copy(k).start())

    each(C - 1, lambda c: subtract(c + 1))

    resid_load.start()
    each(C, lambda c: weight_load(c).start())

    def relay(c):
        @pl.when((tp >= 1) & ((tp != 2) | (c < C - 1)))
        def _():
            diff_copy(tp - 1, c, 1).wait_recv()

            @pl.when((tp == 2) & (c == C - 2))
            def _():
                diff_copy(0, 0, 1).wait_recv()
                forward(0, 0, 1)

            forward(tp - 1, c, 1)

        @pl.when(tp + 1 < T)
        def _():
            diff_copy(tp + 1, c, -1).wait_recv()

            @pl.when(tp >= 1)
            def _():
                forward(tp + 1, c, -1)

    def await_far(c):
        @pl.when(((tp == 2) & (c > 0)) | ((tp == 3) & (c < C - 2)))
        def _():
            diff_copy(tp - 2, c, 1).wait_recv()

        @pl.when(tp < 2)
        def _():
            diff_copy(tp + 2, c, -1).wait_recv()

    def mean_copy(block, h, send, target):
        place = means.at[lax.rem(block, 2) * outer + block // 2, chunk_rows(h)]
        return remote(place, place, send, mean_recv.at[block, h], (upper * pairs + target, tp))

    def outer_copy(i, h):
        return mean_copy(mine, h, outer_send.at[i, h], lax.rem(chip + i, outer) * 2 + core)

    def inner_copy(i, h):
        block = lax.rem(chip + i, outer) * 2 + core
        return mean_copy(block, h, inner_send.at[i, h], chip * 2 + 1 - core)

    def await_mean(block, h):
        mean_copy(block, h, inner_send.at[0, h], chip * 2 + 1 - core).wait_recv()

    counts[...] = jnp.zeros_like(counts)
    group_ids = lax.broadcasted_iota(jnp.int32, (G, lanes), 0)
    lane_ids = lax.broadcasted_iota(jnp.int32, (L, lanes), 0)

    def count(k):
        ids = patched[k] - seq * units + S * units
        high = ids // L - (S * units) // L
        low = lax.rem(ids, L)
        counts[...] += lax.dot_general(
            jnp.where(high == group_ids, 1.0, 0.0).astype(BF16),
            jnp.where(low == lane_ids, 1.0, 0.0).astype(BF16),
            NT, preferred_element_type=F32,
        )

    def spread(g):
        row = jnp.broadcast_to(counts[pl.ds(g, 1), :], (128, L))
        mask[pl.ds(pl.multiple_of(g * L, 8), L), :] = row.T

    def average(k):
        grad_copy(k).wait_recv()
        r = chunk_rows(k)
        both = grad[r, :].astype(F32) + partner_grad[r, :].astype(F32)
        means[core * outer + chip, r, :] = (both * 0.5).astype(BF16)
        each(outer - 1, lambda i: outer_copy(i + 1, k).start())
        inner_copy(0, k).start()

        @pl.when(leads & (k == 2))
        def _():
            pl.semaphore_signal(
                turn, inc=1, device_id=(sibling, tp), device_id_type=pl.DeviceIdType.MESH
            )

    def pass_on(k):
        def step(i):
            await_mean(lax.rem(chip + i + 1, outer) * 2 + core, k)
            inner_copy(i + 1, k).start()

        each(outer - 1, step)

    ids = patched.shape[0]
    ahead = max(ids - K, 0)
    each(ids, lambda k: ids_load(k).wait())
    each(ahead, count)

    @pl.when(follows)
    def _():
        pl.semaphore_wait(turn, 1)
        each(K, lambda k: grad_copy(k).start())

    def count_beside(k):
        @pl.when(ahead + k < ids)
        def _():
            count(ahead + k)

    for k in range(2):
        average(k)
        count_beside(k)

    def average_and_pass(k):
        average(k + 2)

        @pl.when(~follows)
        def _():
            pass_on(k)

        count_beside(k + 2)

    each(K - 2, average_and_pass)
    resid_load.wait()
    resid_copy.start()
    each(C // 2, relay)

    @pl.when(~follows)
    def _():
        each(G, spread)

    acc[...] = jnp.zeros_like(acc)
    token[...] = jnp.zeros_like(token)

    def await_inner(k):
        each(outer, lambda i: await_mean(lax.rem(chip + i, outer) * 2 + 1 - core, k))

    @pl.when(~follows)
    def _():
        pass_on(K - 2)
        pass_on(K - 1)

    @pl.when(follows)
    def _():
        each(K, await_inner)

    far = jnp.where(tp == 0, T - 1, 0)
    inward = jnp.where(tp == 0, 1, -1)

    def partial_copy(c):
        r = piece_rows(c)
        return remote(
            partial.at[r], partial_in.at[r], part_send.at[c], part_recv.at[c], (seq, tp + inward)
        )

    def multiply(side, c):
        r = piece_rows(c)
        right = means[pl.ds(side * outer, outer)]
        right = right.reshape(outer * rows, right.shape[-1])
        result = lax.dot_general(weight[r, :], right, NT, preferred_element_type=F32)
        for j in range(outer):
            part = result[:, j * rows : (j + 1) * rows]
            if single:
                unit[2 * j + side, r, :] = part
            else:
                place = (2 * j + side) * rows
                columns = pl.ds(pl.multiple_of(lax.rem(place, local_len), 128), rows)
                unit[place // local_len, r, columns] = part

    def export(block, source, slot):
        partial[piece_rows(slot), :] = unit[block, piece_rows(source), :].astype(BF16)
        partial_copy(slot).start()

    def ship(c):
        @pl.when((tp == 0) | ((tp == T - 1) & (c > 0)))
        def _():
            export(far, c, c)

    def multiply_first(c):
        weight_load(c).wait()
        multiply(first, c)
        if single:
            ship(c)

        @pl.when(follows)
        def _():
            pass_on(c)

    each(C // 2, multiply_first)

    def multiply_and_relay(c):
        multiply_first(c + C // 2)
        relay(c + C // 2)

    each(C - C // 2, multiply_and_relay)

    per = G // C
    kept = G - per

    def slice_rows(g):
        return pl.ds((kept + g) * L, L)

    def slice_copy(g):
        place = diff.at[1, slice_rows(g)]
        return remote(place, place, slice_send.at[g], slice_recv.at[g], (seq, 2))

    @pl.when(tp == 1)
    def _():
        for g in range(per):
            slice_copy(g).start()

    @pl.when(follows)
    def _():
        each(K - C, lambda k: pass_on(k + C))
        each(G, spread)

    @pl.when(~follows)
    def _():
        each(K, await_inner)

    def multiply_second(c):
        multiply(1 - first, c)
        if not single:
            ship(c)

        @pl.when((tp == T - 1) & (c == C - 1))
        def _():
            export(1, C - 1, 0)

    each(C, multiply_second)

    def product(block, c):
        product_rows(block, piece_rows(c))

    def product_rows(block, r):
        value = diff[block, r, :].astype(F32) * unit[block, r, :]
        masks = mask[r, :]
        for k in range(local_len // 128):
            part = value[:, k * 128 : (k + 1) * 128]
            acc[r, :] += part
            token[block, :, k * 128 : (k + 1) * 128] += jnp.sum(
                part * masks, axis=0, keepdims=True
            )

    def products(s, c):
        if s == 0:
            product(tp, c)
            return

        if s == 1:
            left = (tp >= 1) & ((tp != 2) | (c < C - 1))
        else:
            left = (tp == 2) | ((tp == 3) & (c < C - 2))

        @pl.when(left)
        def _():
            product(tp - s, c)

        @pl.when(tp + s < T)
        def _():
            product(tp + s, c)

    resid_copy.wait()
    sign = (1 - 2 * upper).astype(F32)

    difference = sign * (resid[keep, :].astype(F32) - partner_resid[...].astype(F32))

    def score(gradient):
        terms = difference * gradient.astype(F32)
        folded = terms[:, 0:128]
        for j in range(1, terms.shape[1] // 128):
            folded = folded + terms[:, j * 128 : (j + 1) * 128]
        return jnp.sum(folded.T, axis=0, keepdims=True)

    score_out[...] = score(partner_grad[keep, :])
    score_copy.start()
    scored[upper] = score(grad[keep, :])
    each(C, lambda c: products(0, c))
    each(C, lambda c: products(1, c))
    def await_help(slot):
        part = piece_rows(slot)
        remote(
            partial.at[part], partial_in.at[part], part_send.at[slot], part_recv.at[slot],
            (seq, jnp.where(tp == 1, 0, T - 1)),
        ).wait_recv()

    def help_in(c):
        @pl.when((tp == 1) | ((tp == 2) & (c > 0)))
        def _():
            await_help(c)
            r = piece_rows(c)
            unit[jnp.where(tp == 1, T - 1, 0), r, :] += partial_in[r, :].astype(F32)

    def fold(g, target, row):
        block = acc[pl.ds(pl.multiple_of(g * L, 8), L), :]
        target[pl.ds(row, 1), :] = jnp.sum(block.T, axis=0, keepdims=True)

    score_copy.wait()
    message[kept:, :] = jnp.zeros((2, L), F32)
    for k in range(2):
        message[kept + k : kept + k + 1, 0:half] = scored[k]

    me = seq * T + tp
    other = jnp.where(tp == 3, 2, tp + 1)
    middle = jnp.where(tp == 0, 3, 0)
    late = jnp.where(tp < 2, tp + 2, 1)

    def token_copy(s, block):
        return remote(
            token.at[block], token_in.at[me], tok_send.at[0], tok_recv.at[0], (s, block)
        )

    def send_tokens(block):
        each(S, lambda i: token_copy(lax.rem(seq + i, S), block).start())

    each(S - 1, lambda i: token_copy(lax.rem(seq + i + 1, S), tp).start())
    send_tokens(other)

    @pl.when(tp < 2)
    def _():
        send_tokens(middle)

    token_in[me] = token[tp]

    def last(c):
        await_far(c)
        help_in(c)
        products(2, c)

    def last_and_fold(c):
        last(c)
        each(per, lambda g: fold(c * per + g, message, c * per + g))

    def sent_means(k):
        grad_copy(k).wait_send()
        each(outer - 1, lambda i: outer_copy(i + 1, k).wait_send())
        each(outer, lambda i: inner_copy(i, k).wait_send())

    def drain_own(c):
        @pl.when((tp < T - 1) & ((tp != 1) | (c < C - 1)))
        def _():
            diff_copy(tp, c, 1).wait_send()

        @pl.when(tp > 0)
        def _():
            diff_copy(tp, c, -1).wait_send()

    def drain_relay(c):
        @pl.when((tp == 1) | ((tp == 2) & (c < C - 1)))
        def _():
            diff_copy(tp - 1, c, 1).wait_send()

        @pl.when((tp == 1) | (tp == 2))
        def _():
            diff_copy(tp + 1, c, -1).wait_send()

    each(K, sent_means)
    each(C, drain_own)
    each(C - 1, last_and_fold)

    def share(source, target, send, recv, i):
        return remote(source, target.at[tp], send.at[i], recv.at[tp], (seq, lax.rem(tp + i, T)))

    def message_copy(i):
        return share(message, message_in, msg_send, msg_recv, i)

    def ending_copy(i):
        return share(ending, ending_in, end_send, end_recv, i)

    def send_message():
        each(T - 1, lambda i: message_copy(i + 1).start())

    @pl.when(tp < 3)
    def _():
        send_message()

    def send_ending():
        each(T - 1, lambda i: ending_copy(i + 1).start())

    def end(group):
        for g in range(per):
            fold(group + g, ending, g)
        send_ending()

    last(C - 1)

    @pl.when(tp == 2)
    def _():
        send_tokens(0)
        await_help(0)
        unit[1, piece_rows(C - 1), :] += partial_in[piece_rows(0), :].astype(F32)
        for g in range(per):
            slice_copy(g).wait_recv()
            product_rows(1, slice_rows(g))
            fold(kept + g, ending, g)
        send_ending()

    @pl.when(tp == 3)
    def _():
        diff_copy(0, 0, 1).wait_recv()
        product(0, 0)
        send_tokens(0)
        for g in range(per):
            fold(g, message, g)
            fold(kept + g, message, kept - per + g)
        send_message()
        diff_copy(1, C - 2, 1).wait_recv()
        product(1, C - 2)
        end(kept - per)

    @pl.when(tp < 2)
    def _():
        end(kept)

    send_tokens(late)
    message_in[tp] = message[...]
    ending_in[tp] = ending[...]

    @pl.when(at_end)
    def _():
        each(C, lambda c: partial_copy(c).wait_send())

    each(C, drain_relay)

    @pl.when(tp == 1)
    def _():
        for g in range(per):
            slice_copy(g).wait_send()

    @pl.when(tp == 2)
    def _():
        diff_copy(0, 0, 1).wait_send()

    def await_message(i):
        source = lax.rem(tp + i + 1, T)
        remote(
            message, message_in.at[source], msg_send.at[0], msg_recv.at[source], (seq, source)
        ).wait_recv()

    each(T - 1, await_message)
    total = jnp.sum(message_in[...], axis=0)
    split = kept - per
    scores[0:split, :] = total[:split] * scales[2]
    scores[G : G + 2, :] = total[kept:] * scales[0]

    each(T - 1, lambda i: message_copy(i + 1).wait_send())

    def await_ending(i):
        source = lax.rem(tp + i + 1, T)
        remote(
            ending, ending_in.at[source], end_send.at[0], end_recv.at[source], (seq, source)
        ).wait_recv()

    each(T - 1, await_ending)
    rest = jnp.sum(message_in[0:3, split:kept, :], axis=0) + ending_in[3]
    scores[split:kept, :] = rest * scales[2]
    rest = jnp.sum(ending_in[0:3], axis=0) + message_in[3, split:kept, :]
    scores[kept:G, :] = rest * scales[2]
    others = token_in.at[pl.ds(0, S * T - 1)]
    tokens = remote(others, others, tok_send.at[0], tok_recv.at[0], (seq, tp))
    tokens.wait_recv()
    token_total = jnp.sum(token_in[...], axis=0) * scales[1]
    for k in range(local_len // L):
        scores[G + 2 + k : G + 3 + k, :] = token_total[:, k * L : (k + 1) * L]

    tokens.wait_send()
    each(T - 1, lambda i: ending_copy(i + 1).wait_send())


def write(G, K, L, half, scores, resid_out, token_out, neuron_out):
    for k in range(2):
        resid_out[k * half : (k + 1) * half] = scores[G + k, 0:half]
    for k in range(K):
        token_out[k * L : (k + 1) * L] = scores[G + 2 + k, :]
    for g in range(G):
        neuron_out[g * L : (g + 1) * L] = scores[g, :]


def shards(grad_out, resid_in, down_weight, hidden_clean, hidden_corrupt, patched):
    S = lax.axis_size("seq")
    T = lax.axis_size("tp")
    rows, width = grad_out.shape
    units, local_len = hidden_clean.shape
    L = math.gcd(units, 128)
    G = units // L
    C = max(c for c in range(1, 9) if G % c == 0)
    lanes = math.gcd(patched.shape[0], 1024)
    half = rows // 2
    scales = (
        1.0 / math.sqrt(width * T),
        1.0 / math.sqrt(patched.shape[0]),
        1.0 / math.sqrt(local_len * T),
    )
    dma = lambda *shape: pltpu.SemaphoreType.DMA(shape)
    K = local_len // L
    chunks = rows // 16
    scores = pl.pallas_call(
        functools.partial(kernel, S, T, C, G, L, chunks, scales),
        out_shape=pltpu.VMEM((G + 2 + K, L), F32),
        in_specs=[pl.BlockSpec(memory_space=pl.ANY)] * 6,
        out_specs=pl.BlockSpec(memory_space=pltpu.VMEM),
        scratch_shapes=[
            pltpu.VMEM((rows, width), BF16),
            pltpu.VMEM((rows, width), BF16),
            pltpu.VMEM((units, width), BF16),
            pltpu.VMEM((units, local_len), BF16),
            pltpu.VMEM((units, local_len), BF16),
            pltpu.VMEM((patched.shape[0] // lanes, 1, lanes), jnp.int32),
            pltpu.VMEM((rows, width), BF16),
            pltpu.VMEM((half, width), BF16),
            pltpu.VMEM((S // 2, rows, width), BF16),
            pltpu.VMEM((T, units, local_len), BF16),
            pltpu.VMEM((T, units, local_len), F32),
            pltpu.VMEM((units, local_len), BF16),
            pltpu.VMEM((units, local_len), BF16),
            pltpu.VMEM((units, 128), F32),
            pltpu.VMEM((units, 128), F32),
            pltpu.VMEM((T, 1, local_len), F32),
            pltpu.VMEM((S * T, 1, local_len), F32),
            pltpu.VMEM((G - G // C + 2, L), F32),
            pltpu.VMEM((T, G - G // C + 2, L), F32),
            pltpu.VMEM((G // C, L), F32),
            pltpu.VMEM((T, G // C, L), F32),
            pltpu.VMEM((G, L), F32),
            pltpu.VMEM((2, 1, half), F32),
            pltpu.VMEM((1, half), F32),
            dma(2 + patched.shape[0] // lanes), dma(2, C), dma(C), dma(chunks + 2), dma(chunks + 2),
            dma(S // 4, chunks), dma(S // 4, chunks), dma(S // 2, chunks),
            dma(2, T, C), dma(T, C), dma(C), dma(C),
            dma(T), dma(T), dma(T), dma(T), dma(1), dma(1),
            pltpu.SemaphoreType.REGULAR, dma(G // C), dma(G // C),
        ],
        compiler_params=pltpu.CompilerParams(
            collective_id=0, has_side_effects=True, vmem_limit_bytes=56 * 1024 * 1024
        ),
    )(
        grad_out, resid_in, down_weight, hidden_clean, hidden_corrupt,
        patched,
    )
    return pl.pallas_call(
        functools.partial(write, G, K, L, half),
        out_shape=(
            jax.ShapeDtypeStruct((rows,), F32),
            jax.ShapeDtypeStruct((local_len,), F32),
            jax.ShapeDtypeStruct((units,), F32),
        ),
        in_specs=[pl.BlockSpec(memory_space=pltpu.VMEM)],
        out_specs=[pl.BlockSpec(memory_space=pltpu.VMEM)] * 3,
    )(pltpu.with_memory_space_constraint(scores, pltpu.VMEM))


def solution(mesh):
    in_specs = (P("seq", "tp"), P("seq", "tp"), P("seq", "tp"), P("seq", "tp"), P("seq", "tp"), P())
    out_specs = (P("seq"), P("tp"), P("seq"))
    return jax.shard_map(shards, mesh=mesh, in_specs=in_specs, out_specs=out_specs, check_vma=False)
```
